32 devices in a mesh: groups: 2 (over x), lon: 16 (over z, y, core).
Axes of the slice: x: 2, y: 2, z: 4, core: 2. Of those that a mesh axis runs over, the one named last changes fastest.
Arguments:
- state_in: bfloat16 [128, 768, 256], P('groups', 'lon'), parts along dimension 0, may hold values from -6 to 6
- target: bfloat16 [128, 768, 256], P('groups', 'lon'), parts along dimension 0, may hold values from -6 to 6
- ocean_mask: int32 [128, 768], P('groups', 'lon'), parts along dimension 0, may hold values from 0 to 1, as said below
- kernel_one: bfloat16 [3, 3, 256, 256], replicated, may hold values from -0.125 to 0.125
- kernel_two: bfloat16 [3, 3, 256, 256], replicated, may hold values from -0.125 to 0.125
Outputs:
- prediction: bfloat16 [128, 768, 256], P('groups', 'lon'), parts along dimension 0
- grad_one: float32 [6, 3, 256, 256], P('groups'), parts along dimension 0
- grad_two: float32 [6, 3, 256, 256], P('groups'), parts along dimension 0
The draws below stay inside these ranges and needn't reach their ends.
There are 2 independent parts, one for each index of `groups`. The reference program is written for one: setup_inputs(seed, part) draws one part's arguments, and reference() takes and returns one part's arrays. A program takes and returns all parts, laid end to end along the dimension named above; an argument that names none is the same for every part. Nothing has to cross between parts.
Inputs may be any that keep to these rules, and one draw needn't show every extreme that they name: `ocean_mask`: 1 marks an ocean cell and 0 a land cell.
All inputs are finite; a program needn't handle non-finite values.
Results may differ from the reference program's by a relative error of at most 0.02.
Values may be sent and summed in bfloat16 or wider, within the bound.
No kernel may reach another device: no remote copies, remote signals or barrier semaphores. Data moves between devices by JAX's collectives and lax.ppermute only.
A program may use at most 192 MiB of HBM per device.

```python
import math
import jax
import jax.numpy as jnp
from jax import lax

C = 256
LAT = 64
NLON = 768


def draw_ocean_mask(key, part):
    first_key, second_key = jax.random.split(jax.random.fold_in(key, 11))
    coast = jax.random.randint(first_key, (NLON,), 0, 3 * LAT // 4)
    islands = jax.random.randint(second_key, (LAT, NLON), 0, 6)
    rows = lax.broadcasted_iota(jnp.int32, (LAT, NLON), 0)
    return ((rows >= coast[None, :]) & (islands != 0)).astype(jnp.int32)


def block_levels(own_key, extent, shards, low, high):
    loudness = 1.0
    for axis_at, parts in shards:
        draws = jax.random.uniform(jax.random.fold_in(jax.random.fold_in(own_key, 6), axis_at), (parts,), jnp.float32, low / len(shards), high / len(shards))
        loudness = loudness * jnp.repeat(jnp.exp(draws), extent[axis_at] // parts).reshape((-1,) + (1,) * (len(extent) - 1 - axis_at))
    return loudness


def normal_values(own_key, dims, scale, reach, shards=(), held_as=jnp.bfloat16):
    result = jax.random.normal(own_key, dims, jnp.float32) * scale
    if len(shards) > 0:
        result = block_levels(own_key, dims, shards, -0.22, 0.18) * result
    return jnp.clip(result, min=-reach, max=reach).astype(held_as)


def setup_inputs(seed: int = 0, part: int = 0) -> dict:
    key_list = jax.random.split(jax.random.key(seed), 6)
    part_splits = jax.random.split(jax.random.fold_in(key_list[5], part), 6)
    return {
        "state_in": normal_values(part_splits[0], (LAT, NLON, C), 1.0, 6.0, ((1, 16),)),
        "target": normal_values(part_splits[1], (LAT, NLON, C), 1.0, 6.0, ((1, 16),)),
        "ocean_mask": draw_ocean_mask(jax.random.fold_in(jax.random.fold_in(key_list[5], part), 71), part),
        "kernel_one": normal_values(key_list[3], (3, 3, C, C), (9 * C) ** -0.5, 0.125),
        "kernel_two": normal_values(key_list[4], (3, 3, C, C), (9 * C) ** -0.5, 0.125),
    }


def extend(values_in):
    wrapped = jnp.concatenate([values_in[:, -1:], values_in, values_in[:, :1]], axis=1)
    return jnp.concatenate([jnp.zeros_like(wrapped[:1]), wrapped, wrapped[-1:, ::-1]], axis=0)

def convolve(padded, kernel):
    height = padded.shape[0] - 2
    width = padded.shape[1] - 2
    channels = padded.shape[2]
    total = jnp.zeros((height * width, kernel.shape[3]), jnp.float32)
    for a in range(3):
        for b in range(3):
            piece = padded[a:a + height, b:b + width].reshape(height * width, channels)
            total = total + jnp.dot(piece, kernel[a, b], preferred_element_type=jnp.float32, precision=lax.Precision.HIGHEST)
    return total.reshape(height, width, kernel.shape[3])

def kernel_grad(padded, error_map):
    height = padded.shape[0] - 2
    width = padded.shape[1] - 2
    channels = padded.shape[2]
    flat_error = error_map.reshape(height * width, channels)
    blocks = []
    for a in range(3):
        for b in range(3):
            piece = padded[a:a + height, b:b + width].reshape(height * width, channels)
            blocks.append(lax.dot_general(piece, flat_error, (((0,), (0,)), ((), ())), preferred_element_type=jnp.float32))
    return jnp.stack(blocks).reshape(3, 3, channels, flat_error.shape[1])

def gelu_value(u):
    return u * 0.5 * (1.0 + jax.scipy.special.erf(u / math.sqrt(2.0)))

def gelu_slope(u):
    return 0.5 * (1.0 + jax.scipy.special.erf(u / math.sqrt(2.0))) + u * jnp.exp(-0.5 * u * u) / math.sqrt(2.0 * math.pi)

def reference(state_in, target, ocean_mask, kernel_one, kernel_two):
    is_ocean = ocean_mask[..., None] == 1
    oceanic = ocean_mask[..., None].astype(jnp.float32)
    masked = jnp.where(is_ocean, state_in, jnp.zeros_like(state_in))
    padded_one = extend(masked)
    pre_act = convolve(padded_one, kernel_one).astype(jnp.bfloat16)
    pre_value = pre_act.astype(jnp.float32)
    hidden = (gelu_value(pre_value) * oceanic).astype(jnp.bfloat16)
    padded_two = extend(hidden)
    output = convolve(padded_two, kernel_two)
    prediction = (output * oceanic).astype(jnp.bfloat16)
    error_scale = 1.0 / math.sqrt(LAT * NLON)
    error_map = (oceanic * (output - target.astype(jnp.float32)) * error_scale).astype(jnp.bfloat16)
    grad_two = kernel_grad(padded_two, error_map)
    kernel_wide = kernel_two.astype(jnp.float32)
    unused, pullback = jax.vjp(lambda hidden_wide: convolve(extend(hidden_wide), kernel_wide), hidden.astype(jnp.float32))
    hidden_grad = pullback(error_map.astype(jnp.float32))[0]
    pre_grad = (hidden_grad * gelu_slope(pre_value) * oceanic).astype(jnp.bfloat16)
    grad_one = kernel_grad(padded_one, pre_grad)
    return (prediction, grad_one, grad_two)
```

```python
import functools
import math

import jax
import jax.numpy as jnp
from jax import lax
from jax.experimental import pallas as pl
from jax.experimental.pallas import tpu as pltpu
from jax.sharding import PartitionSpec as P

F32 = jnp.float32
BF16 = jnp.bfloat16

ERF_NUM = (
    0.00022905065861350646,
    0.0034082910107109506,
    0.050955695062380861,
    0.18520832239976145,
    1.128379143519084,
)
ERF_DEN = (
    -1.1791602954361697e-7,
    0.000023547966471313185,
    0.0010179625278914885,
    0.014070470171167667,
    0.11098505178285362,
    0.49746925110067538,
    1.0,
)


def erf(x):
    x = jnp.clip(x, -3.832506856900711, 3.832506856900711)
    s = x * x
    num = jnp.full_like(s, ERF_NUM[0])
    for k in ERF_NUM[1:]:
        num = num * s + k
    den = jnp.full_like(s, ERF_DEN[0])
    for k in ERF_DEN[1:]:
        den = den * s + k
    return x * num / den


def gelu_pair(u):
    half = 0.5 * (1.0 + erf(u * math.sqrt(0.5)))
    return u * half, half + u * jnp.exp(-0.5 * u * u) * (1.0 / math.sqrt(2.0 * math.pi))


def twice(m):
    return jnp.concatenate([m, m], axis=1)


def span(start, size, step=64):
    return pl.ds(pl.multiple_of(start * step, step), size * step)


def tap_rows(ref, col, cols):
    return jnp.concatenate(
        [ref[a, span(col + b, cols), :] for a in range(3) for b in range(3)], axis=1
    )


def shifted(v, north):
    at = lax.broadcasted_iota(jnp.int32, v.shape, 0)
    up = jnp.where(at == 0, 0.0, pltpu.roll(v, 1, 0))
    down = jnp.where(at == v.shape[0] - 1, north, pltpu.roll(v, v.shape[0] - 1, 0))
    return up, down


def forward_kernel(scale, width, state, target, mask, halo, rows3, mask_north, w_one, w_two,
                   pred, err3, slope, hid3, in3, wide_low, wide_high, acc_a, acc_b, hid_north):
    cols = width + 2

    def put(ref, col, v, north):
        up, down = shifted(v, north)
        ref[0, span(col, 1), :] = up.astype(BF16)
        ref[1, span(col, 1), :] = v.astype(BF16)
        ref[2, span(col, 1), :] = down.astype(BF16)

    def strided(col):
        at = pl.ds(col, 64, stride=width)
        return jnp.concatenate([wide_low[at, :], wide_high[at, :]], axis=1)

    def widen_all(src):
        rows = 192
        def step(i, carry):
            at = pl.ds(pl.multiple_of(i * rows, rows), rows)
            wide_low[at, :] = src[at, 0:128].astype(F32)
            wide_high[at, :] = src[at, 128:256].astype(F32)
            return carry
        lax.fori_loop(0, src.shape[0] // rows, step, 0)

    widen_all(state)
    for i, col in enumerate((0, 1, width + 2, width + 3)):
        put(in3, col, halo[span(i, 1), :].astype(F32), rows3[1, pl.ds(col, 1), :])

    def own(c, carry):
        v = strided(c)
        m = mask[span(c + 1, 1), :].astype(F32)
        put(in3, c + 2, v * twice(m), rows3[1, pl.ds(c + 2, 1), :])
        return carry
    lax.fori_loop(0, width, own, 0, unroll=2)

    lhs = jnp.concatenate(
        [rows3[a, pl.ds(2 - b, 64), :].astype(BF16) for a in range(3) for b in range(3)], axis=1
    )
    u = jnp.dot(lhs, w_one[...], preferred_element_type=F32).astype(BF16).astype(F32)
    hid_north[...] = (gelu_pair(u)[0] * twice(mask_north[...])).astype(BF16).astype(F32)

    n1 = 5

    def conv_one(j, acc):
        acc[0 : n1 * 64, :] = jnp.dot(tap_rows(in3, j * n1, n1), w_one[...], preferred_element_type=F32)

    def act(j, acc):
        for i in range(n1):
            col = j * n1 + i
            u = acc[i * 64 : i * 64 + 64, :].astype(BF16).astype(F32)
            m = twice(mask[span(col, 1), :].astype(F32))
            value, grad = gelu_pair(u)
            slope[span(col, 1), :] = (grad * m).astype(BF16)
            h = (value * m).astype(BF16).astype(F32)
            put(hid3, col, h, hid_north[pl.ds(col, 1), :])

    blocks = cols // n1
    conv_one(0, acc_a)

    def pair_one(t, carry):
        conv_one(2 * t + 1, acc_b)
        act(2 * t, acc_a)
        conv_one(2 * t + 2, acc_a)
        act(2 * t + 1, acc_b)
        return carry
    lax.fori_loop(0, blocks // 2 - 1, pair_one, 0)
    conv_one(blocks - 1, acc_b)
    act(blocks - 2, acc_a)
    act(blocks - 1, acc_b)

    n2 = 4
    widen_all(target)

    def conv_two(j, acc):
        acc[0 : n2 * 64, :] = jnp.dot(tap_rows(hid3, j * n2, n2), w_two[...], preferred_element_type=F32)

    def loss(j, acc):
        for i in range(n2):
            c = j * n2 + i
            o = acc[i * 64 : i * 64 + 64, :]
            m = twice(mask[span(c + 1, 1), :].astype(F32))
            at = pl.ds(c, 64, stride=width)
            t = strided(c)
            p = o * m
            wide_low[at, :] = p[:, 0:128]
            wide_high[at, :] = p[:, 128:256]
            e = (m * (o - t) * scale).astype(BF16).astype(F32)
            up, down = shifted(e, 0.0)
            err3[0, span(c + 1, 1), :] = down.astype(BF16)
            err3[1, span(c + 1, 1), :] = e.astype(BF16)
            err3[2, span(c + 1, 1), :] = up.astype(BF16)

    for col in (0, width + 1):
        err3[1, span(col, 1), :] = jnp.zeros((64, 256), BF16)
    blocks = width // n2
    conv_two(0, acc_a)

    def pair_two(t, carry):
        conv_two(2 * t + 1, acc_b)
        loss(2 * t, acc_a)
        conv_two(2 * t + 2, acc_a)
        loss(2 * t + 1, acc_b)
        return carry
    lax.fori_loop(0, blocks // 2 - 1, pair_two, 0)
    conv_two(blocks - 1, acc_b)
    loss(blocks - 2, acc_a)
    loss(blocks - 1, acc_b)

    def narrow(i, carry):
        at = pl.ds(pl.multiple_of(i * 192, 192), 192)
        pred[at, 0:128] = wide_low[at, :].astype(BF16)
        pred[at, 128:256] = wide_high[at, :].astype(BF16)
        return carry
    lax.fori_loop(0, pred.shape[0] // 192, narrow, 0)


def transposed(src, first, dst):
    pairs = dst.shape[1] // 128

    def step(p, carry):
        for a in range(3):
            block = src[a, span(first + 2 * p, 2), :]
            dst[a * 256 : a * 256 + 256, pl.ds(pl.multiple_of(p * 128, 128), 128)] = block.T
        return carry
    lax.fori_loop(0, pairs, step, 0)


def outer(turned, padded, out):
    total = padded.shape[0]
    inner = total - 128
    for b in range(3):
        if b == 0:
            r = jnp.dot(turned[:, 0:inner], padded[64 : 64 + inner, :], preferred_element_type=F32)
        elif b == 1:
            r = jnp.dot(turned[...], padded[...], preferred_element_type=F32)
        else:
            r = jnp.dot(turned[:, 128:total], padded[64 : 64 + inner, :], preferred_element_type=F32)
        for a in range(3):
            k = (3 * a + b) * 256
            out[k : k + 256, :] = r[a * 256 : a * 256 + 256, :].astype(BF16)


def grad_two_kernel(hid3, err3, out, turned):
    transposed(hid3, 0, turned)
    outer(turned, err3.at[1], out)


def back_kernel(width, err3, edges, north, slope, w_two, out, full, w_turned, fold):
    for k in range(9):
        w_turned[k * 256 : k * 256 + 256, :] = w_two[k * 256 : k * 256 + 256, :].T
    rows = 320

    def copy(i, carry):
        at = pl.ds(pl.multiple_of(i * rows, rows), rows)
        for a in range(3):
            full[a, at, :] = err3[a, at, :]
        return carry
    lax.fori_loop(0, full.shape[1] // rows, copy, 0)
    for i, col in enumerate((0, width + 1)):
        e = edges[span(i, 1), :].astype(F32)
        up, down = shifted(e, 0.0)
        full[0, span(col, 1), :] = down.astype(BF16)
        full[1, span(col, 1), :] = e.astype(BF16)
        full[2, span(col, 1), :] = up.astype(BF16)
    lhs = jnp.concatenate([north[pl.ds(b, 48), :].astype(BF16) for b in range(3)], axis=1)
    fold[...] = jnp.dot(lhs, w_turned[6 * 256 : 9 * 256, :], preferred_element_type=F32)
    for col in (0, width + 1):
        out[span(col, 1), :] = jnp.zeros((64, 256), BF16)
    n = 4
    top = lax.broadcasted_iota(jnp.int32, (64, 256), 0) == 63

    def block(j, carry):
        lhs = jnp.concatenate(
            [full[a, span(j * n + 2 - b, n), :] for a in range(3) for b in range(3)], axis=1
        )
        g = jnp.dot(lhs, w_turned[...], preferred_element_type=F32)
        for i in range(n):
            c = j * n + i
            v = g[i * 64 : i * 64 + 64, :]
            v = v + jnp.where(top, fold[pl.ds(c, 1), :], 0.0)
            s = slope[span(c + 1, 1), :].astype(F32)
            out[span(c + 1, 1), :] = (v * s).astype(BF16)
        return carry
    lax.fori_loop(0, width // n, block, 0, unroll=2)


def grad_one_kernel(in3, pre, out, turned):
    transposed(in3, 1, turned)
    outer(turned, pre, out)


VMEM = pl.BlockSpec(memory_space=pltpu.VMEM)


def call(kernel, args, outs, scratch, flops):
    outs = [jax.ShapeDtypeStruct(s, BF16) for s in outs]
    size = sum(x.size * x.dtype.itemsize for x in list(args) + outs)
    return pl.pallas_call(
        kernel,
        out_shape=outs,
        in_specs=[VMEM] * len(args),
        out_specs=[VMEM] * len(outs),
        scratch_shapes=[pltpu.VMEM(s, d) for s, d in scratch],
        cost_estimate=pl.CostEstimate(flops=flops, bytes_accessed=size, transcendentals=0),
    )(*args)


def shift(x, pairs):
    return lax.ppermute(x, "lon", pairs)


def reduce_scatter(x, index, count):
    bit = 1
    while bit < count:
        half = x.shape[0] // 2
        high = (index & bit) != 0
        send = lax.dynamic_slice_in_dim(x, jnp.where(high, 0, half), half, 0)
        keep = lax.dynamic_slice_in_dim(x, jnp.where(high, half, 0), half, 0)
        got = shift(send, [(i, i ^ bit) for i in range(count)])
        x = (keep.astype(F32) + got.astype(F32)).astype(BF16)
        bit *= 2
    return x


def all_gather(x, index, count):
    bit = count // 2
    while bit:
        high = (index & bit) != 0
        got = shift(x, [(i, i ^ bit) for i in range(count)])
        x = jnp.where(high, jnp.concatenate([got, x]), jnp.concatenate([x, got]))
        bit //= 2
    return x


def local(state_in, target, ocean_mask, kernel_one, kernel_two):
    height, width, channels = state_in.shape
    count = lax.axis_size("lon")
    index = lax.axis_index("lon")
    right = [(i, (i + 1) % count) for i in range(count)]
    left = [(i, (i - 1) % count) for i in range(count)]
    mirror = [(i, count - 1 - i) for i in range(count)]
    mirror_low = [(i, (count - i) % count) for i in range(count)]
    mirror_high = [(i, (count - 2 - i) % count) for i in range(count)]

    maskb = ocean_mask.astype(BF16)

    def edge(at, mask_at):
        m = maskb[:, at : at + 2, None]
        cols = jnp.swapaxes(state_in[:, at : at + 2] * m, 0, 1)
        col_mask = jnp.broadcast_to(maskb[:, mask_at][None, :, None], (1, height, channels))
        return jnp.concatenate([cols, col_mask], axis=0)

    low = shift(edge(width - 2, width - 1), right)
    high = shift(edge(0, 0), left)
    own_rows = state_in[height - 2 :] * maskb[height - 2 :, :, None]
    row_mask = jnp.broadcast_to(maskb[height - 1][None, :, None], (1, width, channels))
    strip = jnp.concatenate([own_rows, row_mask], axis=0)
    strip_main = shift(strip, mirror)
    strip_low = shift(strip[:, 0:2], mirror_low)
    strip_high = shift(strip[:, width - 2 :], mirror_high)
    strip_all = jnp.concatenate([strip_high, strip_main, strip_low], axis=1)[:, ::-1]
    own_top = jnp.concatenate([low[0:2, height - 1], own_rows[1], high[0:2, height - 1]], axis=0)
    rows3 = jnp.concatenate([strip_all[0:2], own_top[None]], axis=0).astype(F32)
    rows3 = jnp.pad(rows3, ((0, 0), (0, 72 - rows3.shape[1]), (0, 0)))
    mask_north = jnp.pad(strip_all[2, 1 : width + 3, 0:128].astype(F32), ((0, 14), (0, 0)))
    halo = jnp.concatenate([low[0:2], high[0:2]], axis=0).reshape(4 * height, channels)
    mask_own = jnp.broadcast_to(maskb.T[:, :, None], (width, height, 128))
    mask_full = jnp.concatenate([low[2:3, :, 0:128], mask_own, high[2:3, :, 0:128]], axis=0)
    mask_full = mask_full.reshape((width + 2) * height, 128)

    cells = height * width
    wide_cells = height * (width + 2)
    w_one = kernel_one.reshape(9 * channels, channels)
    w_two = kernel_two.reshape(9 * channels, channels)
    unit = 2 * cells * 9 * channels * channels
    scale = 1.0 / math.sqrt(height * width * count)
    pred, err3, slope, hid3, in3 = call(
        functools.partial(forward_kernel, scale, width),
        (state_in.reshape(cells, channels), target.reshape(cells, channels), mask_full, halo,
         rows3, mask_north, w_one, w_two),
        [(cells, channels), (3, wide_cells, channels), (wide_cells, channels),
         (3, wide_cells, channels), (3, wide_cells + 2 * height, channels)],
        [((cells, 128), F32), ((cells, 128), F32), ((320, channels), F32), ((320, channels), F32),
         ((64, channels), F32)],
        2 * unit,
    )
    err = err3[1]
    err_low = shift(err[width * height : (width + 1) * height], right)
    err_high = shift(err[height : 2 * height], left)
    err_rows = err.reshape(width + 2, height, channels)[1 : width + 1, height - 1]
    top_main = shift(err_rows, mirror)
    top_low = shift(err_rows[0:1], mirror_low)
    top_high = shift(err_rows[width - 1 :], mirror_high)
    (terms_two,) = call(
        grad_two_kernel, (hid3, err3), [(9 * channels, channels)],
        [((3 * channels, wide_cells), BF16)], unit,
    )
    north = jnp.concatenate([top_high, top_main, top_low], axis=0)[::-1].astype(F32)
    north = jnp.pad(north, ((0, 56 - north.shape[0]), (0, 0)))
    edges = jnp.concatenate([err_low, err_high], axis=0)
    (pre,) = call(
        functools.partial(back_kernel, width), (err3, edges, north, slope, w_two),
        [(wide_cells, channels)],
        [((3, wide_cells, channels), BF16), ((9 * channels, channels), BF16),
         ((width, channels), F32)], unit,
    )
    (terms_one,) = call(
        grad_one_kernel, (in3, pre), [(9 * channels, channels)],
        [((3 * channels, wide_cells), BF16)], unit,
    )

    def total(terms):
        out = all_gather(reduce_scatter(terms, index, count), index, count)
        return out.astype(F32).reshape(3, 3, channels, channels)

    return (pred.reshape(height, width, channels), total(terms_one), total(terms_two))


def solution(mesh):
    return jax.shard_map(
        local,
        mesh=mesh,
        in_specs=(P("groups", "lon", None), P("groups", "lon", None), P("groups", "lon"), P(), P()),
        out_specs=(
            P("groups", "lon", None),
            P("groups", None, None, None),
            P("groups", None, None, None),
        ),
        check_vma=False,
    )
```

```python
import functools
import math

import jax
import jax.numpy as jnp
from jax import lax
from jax.experimental import pallas as pl
from jax.experimental.pallas import tpu as pltpu
from jax.sharding import PartitionSpec as P

F32 = jnp.float32
BF16 = jnp.bfloat16

ERF_NUM = (
    0.00022905065861350646,
    0.0034082910107109506,
    0.050955695062380861,
    0.18520832239976145,
    1.128379143519084,
)
ERF_DEN = (
    -1.1791602954361697e-7,
    0.000023547966471313185,
    0.0010179625278914885,
    0.014070470171167667,
    0.11098505178285362,
    0.49746925110067538,
    1.0,
)


def erf(x):
    x = jnp.clip(x, -3.832506856900711, 3.832506856900711)
    s = x * x
    num = jnp.full_like(s, ERF_NUM[0])
    for k in ERF_NUM[1:]:
        num = num * s + k
    den = jnp.full_like(s, ERF_DEN[0])
    for k in ERF_DEN[1:]:
        den = den * s + k
    return x * num / den


def gelu_pair(u):
    half = 0.5 * (1.0 + erf(u * math.sqrt(0.5)))
    return u * half, half + u * jnp.exp(-0.5 * u * u) * (1.0 / math.sqrt(2.0 * math.pi))


def twice(m):
    return jnp.concatenate([m, m], axis=1)


def span(start, size, step=64):
    return pl.ds(pl.multiple_of(start * step, step), size * step)


def tap_rows(ref, col, cols):
    return jnp.concatenate(
        [ref[a, span(col + b, cols), :] for a in range(3) for b in range(3)], axis=1
    )


def shifted(v, north):
    at = lax.broadcasted_iota(jnp.int32, v.shape, 0)
    up = jnp.where(at == 0, 0.0, pltpu.roll(v, 1, 0))
    down = jnp.where(at == v.shape[0] - 1, north, pltpu.roll(v, v.shape[0] - 1, 0))
    return up, down


def strided(low, high, col, width):
    at = pl.ds(col, 64, stride=width)
    return jnp.concatenate([low[at, :], high[at, :]], axis=1)


def widen(src, low, high):
    rows = 192

    def step(i, carry):
        at = pl.ds(pl.multiple_of(i * rows, rows), rows)
        low[at, :] = src[at, 0:128].astype(F32)
        high[at, :] = src[at, 128:256].astype(F32)
        return carry

    lax.fori_loop(0, src.shape[0] // rows, step, 0)


def put(ref, col, v, north):
    up, down = shifted(v, north)
    ref[0, span(col, 1), :] = up.astype(BF16)
    ref[1, span(col, 1), :] = v.astype(BF16)
    ref[2, span(col, 1), :] = down.astype(BF16)


def build_kernel(width, state, mask, in3, low, high):
    widen(state, low, high)

    def own(c, carry):
        put(in3, c + 3, strided(low, high, c, width) * twice(mask[span(c, 1), :]), 0.0)
        return carry

    lax.fori_loop(0, width, own, 0, unroll=4)


def side_mask(side, j):
    lane = (j % 2) * 128
    first = (4 + j // 2) * 64
    return side[first : first + 64, lane : lane + 128].astype(F32)


def side_column(side, j):
    return side[j * 64 : j * 64 + 64, :].astype(F32) * twice(side_mask(side, j))


def flip(rows, used):
    i = lax.broadcasted_iota(jnp.int32, (64, 64), 0)
    k = lax.broadcasted_iota(jnp.int32, (64, 64), 1)
    matrix = jnp.where((i + k == used - 1), 1.0, 0.0).astype(BF16)
    return jnp.dot(matrix, rows, preferred_element_type=F32)


def strip_kernel(width, low, high, state, mask, out, work):
    work[...] = jnp.zeros_like(work)
    for side, first in ((low, 0), (high, width + 3)):
        for j in range(3):
            m = side_mask(side, j)
            v = side[j * 64 : j * 64 + 64, :].astype(F32) * twice(m)
            for a in range(2):
                work[a * 64 + first + j : a * 64 + first + j + 1, :] = v[62 + a : 63 + a, :]
            work[128 + first + j : 128 + first + j + 1, :] = twice(m[63:64, :])
    for a in range(2):
        m = twice(mask[pl.ds(62 + a, width, stride=64), :])
        v = state[(62 + a) * width : (63 + a) * width, :].astype(F32)
        work[a * 64 + 3 : a * 64 + 3 + width, :] = v * m
        if a:
            work[128 + 3 : 128 + 3 + width, :] = m
    out[...] = work[...].astype(BF16)


def conv_kernel(width, in3, w_one, acc):
    n = (width - 2) // 2
    for j in range(2):
        acc[j * n * 64 : (j + 1) * n * 64, :] = jnp.dot(
            tap_rows(in3, 3 + j * n, n), w_one[...], preferred_element_type=F32
        )


def forward_kernel(scale, width, acc, in3_in, target, mask, low, high, strip, strip_own,
                   w_one, w_two, pred, err3, slope, hid3, top_row, in3, t_low, t_high, p_low, p_high,
                   fix, hid_north, acc_a, acc_b, rows3, north_mask, top_work):
    del in3_in
    widen(target, t_low, t_high)
    top = lax.broadcasted_iota(jnp.int32, (64, 256), 0) == 63
    last = lax.broadcasted_iota(jnp.int32, (16, 256), 0) == 15
    blank = jnp.zeros((8, 256), F32)
    for a in range(3):
        rows3[a, 64:72, :] = blank
    rows3[0, 0:64, :] = flip(strip[0:64, :], width + 6)
    rows3[1, 0:64, :] = flip(strip[64:128, :], width + 6)
    rows3[2, 0:64, :] = strip_own[64:128, :].astype(F32)
    north_mask[64:72, :] = blank
    north_mask[0:64, :] = flip(strip[128:192, :], width + 6)
    for j in range(3):
        put(in3, j, side_column(low, j), rows3[1, j : j + 1, :])
        k = width + 3 + j
        put(in3, k, side_column(high, j), rows3[1, k : k + 1, :])
    for c in range(width):
        at = pl.ds((c + 3) * 64 + 48, 16)
        rows = in3[2, at, :].astype(F32)
        in3[2, at, :] = jnp.where(last, rows3[1, pl.ds(c + 3, 1), :], rows).astype(BF16)

    def mask_at(col):
        if col < 2:
            return twice(side_mask(low, col + 1))
        if col >= width + 2:
            return twice(side_mask(high, col - width - 2))
        return twice(mask[(col - 2) * 64 : (col - 1) * 64, :])

    lhs = jnp.concatenate([rows3[1, pl.ds(2 + b, 64), :].astype(BF16) for b in range(3)], axis=1)
    fix[...] = jnp.dot(lhs, w_one[6 * 256 : 9 * 256, :], preferred_element_type=F32)
    lhs = jnp.concatenate(
        [rows3[a, pl.ds(2 - b, 64), :].astype(BF16) for a in range(3) for b in range(3)], axis=1
    )
    lhs = jnp.concatenate([tap_rows(in3, 0, 3), tap_rows(in3, width + 1, 3), lhs], axis=0)
    acc_a[0 : 7 * 64, :] = jnp.dot(lhs, w_one[...], preferred_element_type=F32)
    u = acc_a[6 * 64 : 7 * 64, :].astype(BF16).astype(F32)
    hid_north[...] = (gelu_pair(u)[0] * north_mask[1:65, :]).astype(BF16).astype(F32)

    def act(col):
        c = col - 2
        if c < 1:
            u = acc_a[col * 64 : col * 64 + 64, :]
        elif c > width - 2:
            k = c - (width - 1) + 3
            u = acc_a[k * 64 : k * 64 + 64, :]
        else:
            u = acc[(c - 1) * 64 : c * 64, :] + jnp.where(top, fix[pl.ds(c, 1), :], 0.0)
        u = u.astype(BF16).astype(F32)
        m = mask_at(col)
        value, grad = gelu_pair(u)
        if 0 <= c < width:
            slope[c * 64 : c * 64 + 64, :] = (grad * m).astype(BF16)
        put(hid3, col, (value * m).astype(BF16).astype(F32), hid_north[pl.ds(col, 1), :])

    def loss(e, o):
        c = e - 1
        m = mask_at(e + 1)
        if c < 0:
            t = low[192:256, :].astype(F32)
        elif c >= width:
            t = high[192:256, :].astype(F32)
        else:
            t = strided(t_low, t_high, c, width)
            p = o * m
            at = pl.ds(c, 64, stride=width)
            p_low[at, :] = p[:, 0:128]
            p_high[at, :] = p[:, 128:256]
        v = (m * (o - t) * scale).astype(BF16).astype(F32)
        top_work[e : e + 1, :] = v[63:64, :]
        up, down = shifted(v, 0.0)
        err3[0, span(e, 1), :] = down.astype(BF16)
        err3[1, span(e, 1), :] = v.astype(BF16)
        err3[2, span(e, 1), :] = up.astype(BF16)

    top_work[...] = jnp.zeros_like(top_work)
    n = 10
    blocks = (width + 2) // n
    done = 0
    for j in range(blocks):
        while done < min(j * n + n + 2, width + 4):
            act(done)
            done += 1
        buf = acc_b.at[j % 2]
        buf[...] = jnp.dot(tap_rows(hid3, j * n, n), w_two[...], preferred_element_type=F32)
        if j:
            for i in range(n):
                loss((j - 1) * n + i, acc_b[(j - 1) % 2, i * 64 : i * 64 + 64, :])
    for i in range(n):
        loss((blocks - 1) * n + i, acc_b[(blocks - 1) % 2, i * 64 : i * 64 + 64, :])

    top_row[...] = top_work[...].astype(BF16)

    def narrow(i, carry):
        at = pl.ds(pl.multiple_of(i * 192, 192), 192)
        pred[at, 0:128] = p_low[at, :].astype(BF16)
        pred[at, 128:256] = p_high[at, :].astype(BF16)
        return carry

    lax.fori_loop(0, pred.shape[0] // 192, narrow, 0)


def outer(field, col, rows, send, keep):
    cells = rows.shape[0]
    first_core = lax.axis_index("lon") % 2 == 0
    for a in range(3):
        for b in range(3):
            first = (col + b) * 64
            r = lax.dot_general(
                field[a, first : first + cells, :], rows[...], (((0,), (0,)), ((), ())),
                preferred_element_type=F32,
            )
            at = slice((3 * a + b) * 128, (3 * a + b + 1) * 128)
            keep[at, :] = jnp.where(first_core, r[0:128, :], r[128:256, :]).astype(BF16)
            send[at, :] = jnp.where(first_core, r[128:256, :], r[0:128, :]).astype(BF16)


def grad_two_kernel(width, hid3, err3, send, keep):
    outer(hid3, 1, err3.at[1, 64 : 64 + width * 64], send, keep)


def back_kernel(width, err3, top, slope, w_two, tie, out, w_turned, fold, north):
    del tie
    north[64:72, :] = jnp.zeros((8, 256), F32)
    north[0:64, :] = flip(top[...], width + 2)
    for k in range(9):
        w_turned[k * 256 : k * 256 + 256, :] = w_two[k * 256 : k * 256 + 256, :].T
    lhs = jnp.concatenate([north[pl.ds(b, 64), :].astype(BF16) for b in range(3)], axis=1)
    fold[...] = jnp.dot(lhs, w_turned[6 * 256 : 9 * 256, :], preferred_element_type=F32)
    n = 16
    at_top = lax.broadcasted_iota(jnp.int32, (64, 256), 0) == 63
    for j in range(width // n):
        lhs = jnp.concatenate(
            [err3[a, span(j * n + 2 - b, n), :] for a in range(3) for b in range(3)], axis=1
        )
        g = jnp.dot(lhs, w_turned[...], preferred_element_type=F32)
        for i in range(n):
            c = j * n + i
            v = g[i * 64 : i * 64 + 64, :] + jnp.where(at_top, fold[pl.ds(c, 1), :], 0.0)
            out[span(c, 1), :] = (v * slope[span(c, 1), :].astype(F32)).astype(BF16)


def grad_one_kernel(in3, pre, send, keep):
    outer(in3, 2, pre, send, keep)


def split_kernel(kept, got, own, part_one, part_two, part_three, work):
    place = (lax.axis_index("lon") // 2) % 4
    rows = own.shape[0]
    work[...] = (kept[...].astype(F32) + got[...].astype(F32)).astype(BF16)
    for k, ref in enumerate((own, part_one, part_two, part_three)):
        peer = place ^ k
        ref[...] = work[pl.ds(pl.multiple_of(peer * rows, rows), rows), :]


def finish_kernel(mine, other, out):
    first_core = lax.axis_index("lon") % 2 == 0
    for t in range(9):
        x = mine[t * 128 : t * 128 + 128, :].astype(F32)
        y = other[t * 128 : t * 128 + 128, :].astype(F32)
        out[t * 256 : t * 256 + 128, :] = jnp.where(first_core, x, y)
        out[t * 256 + 128 : t * 256 + 256, :] = jnp.where(first_core, y, x)


VMEM = pl.BlockSpec(memory_space=pltpu.VMEM)
ANY = pl.BlockSpec(memory_space=pl.ANY)


def call(kernel, args, outs, scratch, flops, grant, alias=None, free=()):
    outs = [jax.ShapeDtypeStruct(s, d) for s, d in outs]
    size = sum(x.size * x.dtype.itemsize for x in list(args) + outs)
    return pl.pallas_call(
        kernel,
        out_shape=outs,
        in_specs=[ANY if i in free else VMEM for i in range(len(args))],
        out_specs=[VMEM] * len(outs),
        scratch_shapes=[pltpu.VMEM(s, d) for s, d in scratch],
        input_output_aliases=alias or {},
        compiler_params=pltpu.CompilerParams(vmem_limit_bytes=grant << 20),
        cost_estimate=pl.CostEstimate(flops=flops, bytes_accessed=size, transcendentals=0),
    )(*args)


def shift(x, pairs):
    return lax.ppermute(x, "lon", pairs)


def sum_terms(send, keep, index, count):
    def xor(value, bits):
        return shift(value, [(i, i ^ bits) for i in range(count)])

    half, channels = keep.shape
    rows = half // 4
    got = xor(send, 1)
    own, *parts = call(
        split_kernel, (keep, got), [((rows, channels), BF16)] * 4,
        [((half, channels), BF16)], half * channels, 4,
    )
    parts = [xor(parts[k - 1], 2 * k) for k in (3, 1, 2)]
    x = own.astype(F32) + (parts[0].astype(F32) + (parts[1].astype(F32) + parts[2].astype(F32)))
    x = x.astype(BF16)
    bits = 8
    while bits < count:
        x = (x.astype(F32) + xor(x, bits).astype(F32)).astype(BF16)
        bits *= 2
    parts = [(k, xor(x, 2 * k)) for k in (3, 1, 2)]
    place = (index >> 1) & 3
    whole = jnp.zeros((half, channels), BF16)
    whole = lax.dynamic_update_slice_in_dim(whole, x, place * rows, 0)
    for k, part in parts:
        whole = lax.dynamic_update_slice_in_dim(whole, part, (place ^ k) * rows, 0)
    (out,) = call(
        finish_kernel, (whole, xor(whole, 1)),
        [((2 * half, channels), F32)], [], half * channels, 6,
    )
    return out


def program(state_in, target, ocean_mask, kernel_one, kernel_two):
    height, width, channels = state_in.shape
    count = lax.axis_size("lon")
    index = lax.axis_index("lon")
    right = [(i, (i + 1) % count) for i in range(count)]
    left = [(i, (i - 1) % count) for i in range(count)]
    mirror = [(i, count - 1 - i) for i in range(count)]
    cells = height * width
    w_one = kernel_one.reshape(9 * channels, channels)
    w_two = kernel_two.reshape(9 * channels, channels)
    unit = 2 * cells * 9 * channels * channels
    scale = 1.0 / math.sqrt(height * width * count)

    mask = jnp.broadcast_to(ocean_mask.T[:, :, None].astype(F32), (width, height, 128))

    def edge(at, target_at):
        m = mask[at : at + 3].astype(BF16)
        return jnp.concatenate(
            [jnp.swapaxes(state_in[:, at : at + 3], 0, 1),
             jnp.swapaxes(target[:, target_at : target_at + 1], 0, 1),
             jnp.concatenate([m[0:1], m[1:2]], axis=2), jnp.concatenate([m[2:3], m[2:3]], axis=2)],
            axis=0,
        ).reshape(6 * height, channels)

    low = shift(edge(width - 3, width - 1), right)
    high = shift(edge(0, 0), left)
    state = state_in.reshape(cells, channels)
    mask = mask.reshape(cells, 128)
    (in3,) = call(
        functools.partial(build_kernel, width), (state, mask),
        [((3, (width + 6) * height, channels), BF16)],
        [((cells, 128), F32), ((cells, 128), F32)], unit // 4, 8,
    )
    (strip_own,) = call(
        functools.partial(strip_kernel, width), (low, high, state, mask),
        [((192, channels), BF16)], [((192, channels), F32)], unit // 16, 4,
    )
    strip = shift(strip_own, mirror)
    (acc,) = call(
        functools.partial(conv_kernel, width), (in3, w_one),
        [(((width - 2) * height, channels), F32)], [], unit, 6,
    )
    pred, err3, slope, hid3, top, in3 = call(
        functools.partial(forward_kernel, scale, width),
        (acc, in3, target.reshape(cells, channels), mask, low, high, strip, strip_own, w_one, w_two),
        [((cells, channels), BF16), ((3, (width + 2) * height, channels), BF16),
         ((cells, channels), BF16), ((3, (width + 4) * height, channels), BF16),
         ((64, channels), BF16), (in3.shape, BF16)],
        [((cells, 128), F32)] * 4
        + [((64, channels), F32), ((64, channels), F32), ((448, channels), F32),
           ((2, 640, channels), F32), ((3, 72, channels), F32), ((72, channels), F32),
           ((64, channels), F32)],
        2 * unit, 16, alias={1: 5},
    )
    top = shift(top, mirror)
    terms_two = call(
        functools.partial(grad_two_kernel, width), (hid3, err3),
        [((9 * channels // 2, channels), BF16)] * 2, [], unit, 6,
    )
    (pre,) = call(
        functools.partial(back_kernel, width), (err3, top, slope, w_two, terms_two[1]),
        [((cells, channels), BF16)],
        [((9 * channels, channels), BF16), ((64, channels), F32), ((72, channels), F32)],
        unit, 10, free=(4,),
    )
    terms_one = call(
        grad_one_kernel, (in3, pre), [((9 * channels // 2, channels), BF16)] * 2, [],
        unit, 6,
    )
    shape = (3, 3, channels, channels)
    grad_two = sum_terms(*terms_two, index, count).reshape(shape)
    grad_one = sum_terms(*terms_one, index, count).reshape(shape)
    return (pred.reshape(height, width, channels), grad_one, grad_two)


def solution(mesh):
    return jax.shard_map(
        program,
        mesh=mesh,
        in_specs=(P("groups", "lon", None), P("groups", "lon", None), P("groups", "lon"), P(), P()),
        out_specs=(
            P("groups", "lon", None),
            P("groups", None, None, None),
            P("groups", None, None, None),
        ),
        check_vma=False,
    )
```

```python
import functools
import math

import jax
import jax.numpy as jnp
from jax import lax
from jax.experimental import pallas as pl
from jax.experimental.pallas import tpu as pltpu
from jax.sharding import PartitionSpec as P


F32 = jnp.float32
BF16 = jnp.bfloat16

ERF_NUM = (
    0.00022905065861350646,
    0.0034082910107109506,
    0.050955695062380861,
    0.18520832239976145,
    1.128379143519084,
)
ERF_DEN = (
    -1.1791602954361697e-7,
    0.000023547966471313185,
    0.0010179625278914885,
    0.014070470171167667,
    0.11098505178285362,
    0.49746925110067538,
    1.0,
)


def erf(x):
    x = jnp.clip(x, -3.832506856900711, 3.832506856900711)
    s = x * x
    num = jnp.full_like(s, ERF_NUM[0])
    for k in ERF_NUM[1:]:
        num = num * s + k
    den = jnp.full_like(s, ERF_DEN[0])
    for k in ERF_DEN[1:]:
        den = den * s + k
    return x * num / den


def gelu_pair(u):
    half = 0.5 * (1.0 + erf(u * math.sqrt(0.5)))
    return u * half, half + u * jnp.exp(-0.5 * u * u) * (1.0 / math.sqrt(2.0 * math.pi))


def twice(m):
    return jnp.concatenate([m, m], axis=1)


def span(start, size, step=64):
    return pl.ds(pl.multiple_of(start * step, step), size * step)


def tap_rows(ref, col, cols):
    return jnp.concatenate(
        [ref[a, span(col + b, cols), :] for a in range(3) for b in range(3)], axis=1
    )


def shifted(v, north):
    at = lax.broadcasted_iota(jnp.int32, v.shape, 0)
    up = jnp.where(at == 0, 0.0, pltpu.roll(v, 1, 0))
    down = jnp.where(at == v.shape[0] - 1, north, pltpu.roll(v, v.shape[0] - 1, 0))
    return up, down


def strided(low, high, col, width):
    at = pl.ds(col, 64, stride=width)
    return jnp.concatenate([low[at, :], high[at, :]], axis=1)


def widen(src, low, high):
    rows = 192

    def step(i, carry):
        at = pl.ds(pl.multiple_of(i * rows, rows), rows)
        low[at, :] = src[at, 0:128].astype(F32)
        high[at, :] = src[at, 128:256].astype(F32)
        return carry

    lax.fori_loop(0, src.shape[0] // rows, step, 0)


def put(ref, col, v, north):
    up, down = shifted(v, north)
    ref[0, span(col, 1), :] = up.astype(BF16)
    ref[1, span(col, 1), :] = v.astype(BF16)
    ref[2, span(col, 1), :] = down.astype(BF16)


def pack_kernel(width, state, target, mask_rows, mask, low, high, tiles, rows, part_low, part_high, sems):
    last = width // 16 - 1
    get_mask = pltpu.make_async_copy(mask_rows, rows, sems.at[4])
    get_mask.start()
    copies = []
    for i, (src, tile) in enumerate(((state, last), (target, last), (state, 0), (target, 0))):
        copy = pltpu.make_async_copy(src.at[:, tile * 16 : tile * 16 + 16, :], tiles.at[i], sems.at[i])
        copy.start()
        copies.append(copy)
    get_mask.wait()
    square = jnp.concatenate([rows[...], jnp.zeros((128 - width, 64), jnp.int32)], axis=0)
    turned = square.astype(F32).T
    for c in range(width):
        mask[c * 64 : c * 64 + 64, :] = jnp.broadcast_to(turned[:, c : c + 1], (64, 128))

    def columns(i):
        copies[i].wait()

        def step(r, carry):
            v = tiles[i, r].astype(F32)
            at = pl.ds(pl.multiple_of(r * 16, 16), 16)
            part_low[at, :] = v[:, 0:128]
            part_high[at, :] = v[:, 128:256]
            return carry

        lax.fori_loop(0, 64, step, 0, unroll=8)

    def edge(out, i, first, inner, side):
        columns(i)
        for j in range(3):
            out[j * 64 : j * 64 + 64, :] = strided(part_low, part_high, inner + j, 16).astype(BF16)
        columns(i + 1)
        out[192:256, :] = strided(part_low, part_high, side, 16).astype(BF16)
        m = [mask[(first + j) * 64 : (first + j + 1) * 64, :].astype(BF16) for j in range(3)]
        out[256:320, :] = jnp.concatenate([m[0], m[1]], axis=1)
        out[320:384, :] = jnp.concatenate([m[2], m[2]], axis=1)

    edge(low, 0, width - 3, 13, 15)
    edge(high, 2, 0, 0, 0)


def build_kernel(width, state, mask, in3, low, high):
    widen(state, low, high)

    def own(c, carry):
        put(in3, c + 3, strided(low, high, c, width) * twice(mask[span(c, 1), :]), 0.0)
        return carry

    lax.fori_loop(0, width, own, 0, unroll=4)


def side_mask(side, j):
    lane = (j % 2) * 128
    first = (4 + j // 2) * 64
    return side[first : first + 64, lane : lane + 128].astype(F32)


def side_column(side, j):
    return side[j * 64 : j * 64 + 64, :].astype(F32) * twice(side_mask(side, j))


def flip(rows, used):
    i = lax.broadcasted_iota(jnp.int32, (64, 64), 0)
    k = lax.broadcasted_iota(jnp.int32, (64, 64), 1)
    matrix = jnp.where((i + k == used - 1), 1.0, 0.0).astype(BF16)
    return jnp.dot(matrix, rows, preferred_element_type=F32)


def strip_kernel(width, low, high, state, mask, out, work):
    work[...] = jnp.zeros_like(work)
    for side, first in ((low, 0), (high, width + 3)):
        for j in range(3):
            m = side_mask(side, j)
            v = side[j * 64 : j * 64 + 64, :].astype(F32) * twice(m)
            for a in range(2):
                work[a * 64 + first + j : a * 64 + first + j + 1, :] = v[62 + a : 63 + a, :]
            work[128 + first + j : 128 + first + j + 1, :] = twice(m[63:64, :])
    for a in range(2):
        m = twice(mask[pl.ds(62 + a, width, stride=64), :])
        v = state[(62 + a) * width : (63 + a) * width, :].astype(F32)
        work[a * 64 + 3 : a * 64 + 3 + width, :] = v * m
        if a:
            work[128 + 3 : 128 + 3 + width, :] = m
    out[...] = work[...].astype(BF16)


def conv_kernel(width, in3, w_one, acc):
    n = (width - 2) // 2
    for j in range(2):
        acc[j * n * 64 : (j + 1) * n * 64, :] = jnp.dot(
            tap_rows(in3, 3 + j * n, n), w_one[...], preferred_element_type=F32
        )


def forward_kernel(scale, width, acc, in3_in, target, mask, low, high, strip, strip_own,
                   w_one, w_two, pred, err3, slope, hid3, top_row, in3, t_low, t_high, p_low, p_high,
                   fix, hid_north, acc_a, acc_b, rows3, north_mask, top_work):
    del in3_in
    widen(target, t_low, t_high)
    top = lax.broadcasted_iota(jnp.int32, (64, 256), 0) == 63
    last = lax.broadcasted_iota(jnp.int32, (16, 256), 0) == 15
    blank = jnp.zeros((8, 256), F32)
    for a in range(3):
        rows3[a, 64:72, :] = blank
    rows3[0, 0:64, :] = flip(strip[0:64, :], width + 6)
    rows3[1, 0:64, :] = flip(strip[64:128, :], width + 6)
    rows3[2, 0:64, :] = strip_own[64:128, :].astype(F32)
    north_mask[64:72, :] = blank
    north_mask[0:64, :] = flip(strip[128:192, :], width + 6)
    for j in range(3):
        put(in3, j, side_column(low, j), rows3[1, j : j + 1, :])
        k = width + 3 + j
        put(in3, k, side_column(high, j), rows3[1, k : k + 1, :])
    for c in range(width):
        at = pl.ds((c + 3) * 64 + 48, 16)
        rows = in3[2, at, :].astype(F32)
        in3[2, at, :] = jnp.where(last, rows3[1, pl.ds(c + 3, 1), :], rows).astype(BF16)

    def mask_at(col):
        if col < 2:
            return twice(side_mask(low, col + 1))
        if col >= width + 2:
            return twice(side_mask(high, col - width - 2))
        return twice(mask[(col - 2) * 64 : (col - 1) * 64, :])

    lhs = jnp.concatenate([rows3[1, pl.ds(2 + b, 64), :].astype(BF16) for b in range(3)], axis=1)
    fix[...] = jnp.dot(lhs, w_one[6 * 256 : 9 * 256, :], preferred_element_type=F32)
    lhs = jnp.concatenate(
        [rows3[a, pl.ds(2 - b, 64), :].astype(BF16) for a in range(3) for b in range(3)], axis=1
    )
    lhs = jnp.concatenate([tap_rows(in3, 0, 3), tap_rows(in3, width + 1, 3), lhs], axis=0)
    acc_a[0 : 7 * 64, :] = jnp.dot(lhs, w_one[...], preferred_element_type=F32)
    u = acc_a[6 * 64 : 7 * 64, :].astype(BF16).astype(F32)
    hid_north[...] = (gelu_pair(u)[0] * north_mask[1:65, :]).astype(BF16).astype(F32)

    def act(col):
        c = col - 2
        if c < 1:
            u = acc_a[col * 64 : col * 64 + 64, :]
        elif c > width - 2:
            k = c - (width - 1) + 3
            u = acc_a[k * 64 : k * 64 + 64, :]
        else:
            u = acc[(c - 1) * 64 : c * 64, :] + jnp.where(top, fix[pl.ds(c, 1), :], 0.0)
        u = u.astype(BF16).astype(F32)
        m = mask_at(col)
        value, grad = gelu_pair(u)
        if 0 <= c < width:
            slope[c * 64 : c * 64 + 64, :] = (grad * m).astype(BF16)
        put(hid3, col, (value * m).astype(BF16).astype(F32), hid_north[pl.ds(col, 1), :])

    def loss(e, o):
        c = e - 1
        m = mask_at(e + 1)
        if c < 0:
            t = low[192:256, :].astype(F32)
        elif c >= width:
            t = high[192:256, :].astype(F32)
        else:
            t = strided(t_low, t_high, c, width)
            p = o * m
            at = pl.ds(c, 64, stride=width)
            p_low[at, :] = p[:, 0:128]
            p_high[at, :] = p[:, 128:256]
        v = (m * (o - t) * scale).astype(BF16).astype(F32)
        top_work[e : e + 1, :] = v[63:64, :]
        up, down = shifted(v, 0.0)
        err3[0, span(e, 1), :] = down.astype(BF16)
        err3[1, span(e, 1), :] = v.astype(BF16)
        err3[2, span(e, 1), :] = up.astype(BF16)

    top_work[...] = jnp.zeros_like(top_work)
    n = 10
    blocks = (width + 2) // n
    done = 0
    for j in range(blocks):
        while done < min(j * n + n + 2, width + 4):
            act(done)
            done += 1
        buf = acc_b.at[j % 2]
        buf[...] = jnp.dot(tap_rows(hid3, j * n, n), w_two[...], preferred_element_type=F32)
        if j:
            for i in range(n):
                loss((j - 1) * n + i, acc_b[(j - 1) % 2, i * 64 : i * 64 + 64, :])
    for i in range(n):
        loss((blocks - 1) * n + i, acc_b[(blocks - 1) % 2, i * 64 : i * 64 + 64, :])

    top_row[...] = top_work[...].astype(BF16)

    def narrow(i, carry):
        at = pl.ds(pl.multiple_of(i * 192, 192), 192)
        pred[at, 0:128] = p_low[at, :].astype(BF16)
        pred[at, 128:256] = p_high[at, :].astype(BF16)
        return carry

    lax.fori_loop(0, pred.shape[0] // 192, narrow, 0)


def tap(field, col, t, rows):
    at = pl.ds(pl.multiple_of((col + t % 3) * 64, 64), rows.shape[0])
    return lax.dot_general(
        field[t // 3, at, :], rows[...], (((0,), (0,)), ((), ())), preferred_element_type=F32
    )


def outer_sent(field, col, rows, send, rest):
    first_core = lax.axis_index("lon") % 2 == 0
    at = jnp.where(first_core, 128, 0)
    for i in range(4):
        r = tap(field, col, i + jnp.where(first_core, 5, 0), rows)
        send[pl.ds(pl.multiple_of(at + i * 256, 128), 256), :] = r.astype(BF16)
    r = tap(field, col, 4, rows)
    end = pl.ds(pl.multiple_of(jnp.where(first_core, 0, 1024), 128), 128)
    send[end, :] = jnp.where(first_core, r[128:256, :], r[0:128, :]).astype(BF16)
    rest[...] = jnp.where(first_core, r[0:128, :], r[128:256, :]).astype(BF16)


def outer_kept(field, col, rows, rest, keep):
    first_core = lax.axis_index("lon") % 2 == 0
    at = jnp.where(first_core, 0, 128)
    for i in range(4):
        r = tap(field, col, i + jnp.where(first_core, 0, 5), rows)
        keep[pl.ds(pl.multiple_of(at + i * 256, 128), 256), :] = r.astype(BF16)
    end = pl.ds(pl.multiple_of(jnp.where(first_core, 1024, 0), 128), 128)
    keep[end, :] = rest[...]


def two_sent_kernel(width, hid3, err3, send, rest):
    outer_sent(hid3, 1, err3.at[1, 64 : 64 + width * 64], send, rest)


def two_kept_kernel(width, hid3, err3, rest, keep):
    outer_kept(hid3, 1, err3.at[1, 64 : 64 + width * 64], rest, keep)


def one_sent_kernel(in3, pre, send, rest):
    outer_sent(in3, 2, pre, send, rest)


def one_kept_kernel(in3, pre, rest, keep):
    outer_kept(in3, 2, pre, rest, keep)


def back_kernel(width, err3, top, slope, w_two, tie, out, w_turned, fold, north):
    del tie
    north[64:72, :] = jnp.zeros((8, 256), F32)
    north[0:64, :] = flip(top[...], width + 2)
    for k in range(9):
        w_turned[k * 256 : k * 256 + 256, :] = w_two[k * 256 : k * 256 + 256, :].T
    lhs = jnp.concatenate([north[pl.ds(b, 64), :].astype(BF16) for b in range(3)], axis=1)
    fold[...] = jnp.dot(lhs, w_turned[6 * 256 : 9 * 256, :], preferred_element_type=F32)
    n = 16
    at_top = lax.broadcasted_iota(jnp.int32, (64, 256), 0) == 63
    for j in range(width // n):
        lhs = jnp.concatenate(
            [err3[a, span(j * n + 2 - b, n), :] for a in range(3) for b in range(3)], axis=1
        )
        g = jnp.dot(lhs, w_turned[...], preferred_element_type=F32)
        for i in range(n):
            c = j * n + i
            v = g[i * 64 : i * 64 + 64, :] + jnp.where(at_top, fold[pl.ds(c, 1), :], 0.0)
            out[span(c, 1), :] = (v * slope[span(c, 1), :].astype(F32)).astype(BF16)


def split_kernel(peers, kept, got, *refs):
    *parts, work = refs
    place = (lax.axis_index("lon") // 2) % peers
    rows = parts[0].shape[0]
    work[...] = (kept[...].astype(F32) + got[...].astype(F32)).astype(BF16)
    for k, ref in enumerate(parts):
        ref[...] = work[pl.ds(pl.multiple_of((place ^ k) * rows, rows), rows), :]


def gather_kernel(mine, part_three, part_one, part_two, whole):
    place = (lax.axis_index("lon") // 2) % 4
    rows = mine.shape[0]
    for k, ref in ((0, mine), (3, part_three), (1, part_one), (2, part_two)):
        whole[pl.ds(pl.multiple_of((place ^ k) * rows, rows), rows), :] = ref[...]


def finish_kernel(other_half, half, *refs):
    out, work, sems = refs[-3:]
    core = lax.axis_index("lon") % 2
    core = 1 - core if other_half else core
    rows = half.shape[0]
    chunk = rows // 3
    copies = []
    for i in range(3):
        at = slice(i * chunk, (i + 1) * chunk)
        work[at, :] = half[at, :].astype(F32)
        to = pl.ds(pl.multiple_of(core * rows + i * chunk, chunk), chunk)
        copy = pltpu.make_async_copy(work.at[at, :], out.at[to, :], sems.at[i])
        copy.start()
        copies.append(copy)
    for copy in copies:
        copy.wait()


VMEM = pl.BlockSpec(memory_space=pltpu.VMEM)
ANY = pl.BlockSpec(memory_space=pl.ANY)
HBM = pl.BlockSpec(memory_space=pltpu.HBM)


def call(kernel, args, outs, scratch, flops, grant, alias=None, free=(), free_out=False, away=()):
    outs = [jax.ShapeDtypeStruct(s, d) for s, d in outs]
    size = sum(x.size * x.dtype.itemsize for x in list(args) + outs)
    return pl.pallas_call(
        kernel,
        out_shape=outs,
        in_specs=[ANY if i in free else HBM if i in away else VMEM for i in range(len(args))],
        out_specs=[ANY if free_out else VMEM] * len(outs),
        scratch_shapes=[pltpu.VMEM(*s) if isinstance(s, tuple) else s for s in scratch],
        input_output_aliases=alias or {},
        compiler_params=pltpu.CompilerParams(vmem_limit_bytes=grant << 20),
        cost_estimate=pl.CostEstimate(flops=flops, bytes_accessed=size, transcendentals=0),
    )(*args)


def shift(x, pairs):
    return lax.ppermute(x, "lon", pairs)


def exchange(x, bits, count):
    return shift(x, [(i, i ^ bits) for i in range(count)])


def plus(x, *others):
    total = x.astype(F32)
    for y in others:
        total = total + y.astype(F32)
    return total.astype(BF16)


def split(keep, got, peers):
    half, channels = keep.shape
    return call(
        functools.partial(split_kernel, peers), (keep, got),
        [((half // peers, channels), BF16)] * peers, [((half, channels), BF16)], half * channels, 4,
    )


def along_line(x, count):
    bits = 8
    while bits < count:
        x = plus(x, exchange(x, bits, count))
        bits *= 2
    return x


def finish(mine, other):
    half, channels = mine.shape
    scratch = [((half, channels), F32), pltpu.SemaphoreType.DMA((3,))]
    out = [((2 * half, channels), F32)]
    (total,) = call(
        functools.partial(finish_kernel, False), (mine,), out, scratch,
        half * channels, 4, free_out=True,
    )
    (total,) = call(
        functools.partial(finish_kernel, True), (other, total), out, scratch,
        half * channels, 4, alias={1: 0}, free=(1,), free_out=True,
    )
    return total


def sum_square(keep, got, count):
    own, *parts = split(keep, got, 4)
    got = [exchange(parts[k - 1], 2 * k, count) for k in (3, 1, 2)]
    x = along_line(plus(own, *got), count)
    got = [exchange(x, 2 * k, count) for k in (3, 1, 2)]
    (whole,) = call(gather_kernel, (x, *got), [(keep.shape, BF16)], [], keep.size, 4)
    return finish(whole, exchange(whole, 1, count))


def program(state_in, target, ocean_mask, kernel_one, kernel_two):
    height, width, channels = state_in.shape
    count = lax.axis_size("lon")
    right = [(i, (i + 1) % count) for i in range(count)]
    left = [(i, (i - 1) % count) for i in range(count)]
    mirror = [(i, count - 1 - i) for i in range(count)]
    cells = height * width
    w_one = kernel_one.reshape(9 * channels, channels)
    w_two = kernel_two.reshape(9 * channels, channels)
    unit = 2 * cells * 9 * channels * channels
    scale = 1.0 / math.sqrt(height * width * count)

    state = state_in.reshape(cells, channels)
    target = target.reshape(cells, channels)
    mask, low, high = call(
        functools.partial(pack_kernel, width),
        tuple(
            pltpu.with_memory_space_constraint(x, pltpu.HBM)
            for x in (state_in, target.reshape(state_in.shape), ocean_mask.T)
        ),
        [((cells, 128), F32)] + [((6 * height, channels), BF16)] * 2,
        [((4, height, 16, channels), BF16), ((width, height), jnp.int32)]
        + [((16 * height, 128), F32)] * 2 + [pltpu.SemaphoreType.DMA((5,))],
        unit // 16, 8, away=(0, 1, 2),
    )
    low = shift(low, right)
    high = shift(high, left)
    (in3,) = call(
        functools.partial(build_kernel, width), (state, mask),
        [((3, (width + 6) * height, channels), BF16)],
        [((cells, 128), F32), ((cells, 128), F32)], unit // 4, 8,
    )
    (strip_own,) = call(
        functools.partial(strip_kernel, width), (low, high, state, mask),
        [((192, channels), BF16)], [((192, channels), F32)], unit // 16, 4,
    )
    strip = shift(strip_own, mirror)
    (acc,) = call(
        functools.partial(conv_kernel, width), (in3, w_one),
        [(((width - 2) * height, channels), F32)], [], unit, 6,
    )
    pred, err3, slope, hid3, top, in3 = call(
        functools.partial(forward_kernel, scale, width),
        (acc, in3, target, mask, low, high, strip, strip_own, w_one, w_two),
        [((cells, channels), BF16), ((3, (width + 2) * height, channels), BF16),
         ((cells, channels), BF16), ((3, (width + 4) * height, channels), BF16),
         ((64, channels), BF16), (in3.shape, BF16)],
        [((cells, 128), F32)] * 4
        + [((64, channels), F32), ((64, channels), F32), ((448, channels), F32),
           ((2, 640, channels), F32), ((3, 72, channels), F32), ((72, channels), F32),
           ((64, channels), F32)],
        2 * unit, 16, alias={1: 5},
    )
    top = shift(top, mirror)
    half = ((9 * channels // 2, channels), BF16)
    rest = ((channels // 2, channels), BF16)
    send, tail = call(
        functools.partial(two_sent_kernel, width), (hid3, err3), [half, rest], [],
        unit // 2, 6,
    )
    got_two = exchange(send, 1, count)
    (keep_two,) = call(
        functools.partial(two_kept_kernel, width), (hid3, err3, tail), [half], [],
        unit // 2, 6,
    )
    (pre,) = call(
        functools.partial(back_kernel, width), (err3, top, slope, w_two, keep_two),
        [((cells, channels), BF16)],
        [((9 * channels, channels), BF16), ((64, channels), F32), ((72, channels), F32)],
        unit, 10, free=(4,),
    )
    send, tail = call(one_sent_kernel, (in3, pre), [half, rest], [], unit // 2, 6)
    got_one = exchange(send, 1, count)
    (keep_one,) = call(one_kept_kernel, (in3, pre, tail), [half], [], unit // 2, 6)
    shape = (3, 3, channels, channels)
    grad_two = sum_square(keep_two, got_two, count).reshape(shape)
    grad_one = sum_square(keep_one, got_one, count).reshape(shape)
    return (pred.reshape(height, width, channels), grad_one, grad_two)


def solution(mesh):
    return jax.shard_map(
        program,
        mesh=mesh,
        in_specs=(P("groups", "lon", None), P("groups", "lon", None), P("groups", "lon"), P(), P()),
        out_specs=(
            P("groups", "lon", None),
            P("groups", None, None, None),
            P("groups", None, None, None),
        ),
        check_vma=False,
    )
```

```python
import functools
import math

import jax
import jax.numpy as jnp
from jax import lax
from jax.experimental import pallas as pl
from jax.experimental.pallas import tpu as pltpu
from jax.sharding import PartitionSpec as P


F32 = jnp.float32
BF16 = jnp.bfloat16

ERF_NUM = (
    0.00022905065861350646,
    0.0034082910107109506,
    0.050955695062380861,
    0.18520832239976145,
    1.128379143519084,
)
ERF_DEN = (
    -1.1791602954361697e-7,
    0.000023547966471313185,
    0.0010179625278914885,
    0.014070470171167667,
    0.11098505178285362,
    0.49746925110067538,
    1.0,
)


def erf(x):
    x = jnp.clip(x, -3.832506856900711, 3.832506856900711)
    s = x * x
    num = jnp.full_like(s, ERF_NUM[0])
    for k in ERF_NUM[1:]:
        num = num * s + k
    den = jnp.full_like(s, ERF_DEN[0])
    for k in ERF_DEN[1:]:
        den = den * s + k
    return x * num / den


def gelu_pair(u):
    half = 0.5 * (1.0 + erf(u * math.sqrt(0.5)))
    return u * half, half + u * jnp.exp(-0.5 * u * u) * (1.0 / math.sqrt(2.0 * math.pi))


def twice(m):
    return jnp.concatenate([m, m], axis=1)


def span(start, size, step=64):
    return pl.ds(pl.multiple_of(start * step, step), size * step)


def tap_rows(ref, col, cols):
    return jnp.concatenate(
        [ref[a, span(col + b, cols), :] for a in range(3) for b in range(3)], axis=1
    )


def shifted(v, north):
    at = lax.broadcasted_iota(jnp.int32, v.shape, 0)
    up = jnp.where(at == 0, 0.0, pltpu.roll(v, 1, 0))
    down = jnp.where(at == v.shape[0] - 1, north, pltpu.roll(v, v.shape[0] - 1, 0))
    return up, down


def strided(low, high, col, width):
    at = pl.ds(col, 64, stride=width)
    return jnp.concatenate([low[at, :], high[at, :]], axis=1)


def widen(src, low, high):
    rows = 192

    def step(i, carry):
        at = pl.ds(pl.multiple_of(i * rows, rows), rows)
        low[at, :] = src[at, 0:128].astype(F32)
        high[at, :] = src[at, 128:256].astype(F32)
        return carry

    lax.fori_loop(0, src.shape[0] // rows, step, 0)


def put(ref, col, v, north):
    up, down = shifted(v, north)
    ref[0, span(col, 1), :] = up.astype(BF16)
    ref[1, span(col, 1), :] = v.astype(BF16)
    ref[2, span(col, 1), :] = down.astype(BF16)


def turn_mask(mask_rows):
    blank = jnp.zeros((128 - mask_rows.shape[0], 64), jnp.int32)
    return jnp.concatenate([mask_rows[...], blank], axis=0).astype(F32).T


def pack_kernel(width, state, target, mask_rows, low, high, top, tiles, rows, part_low, part_high, sems):
    last = width // 16 - 1
    get_mask = pltpu.make_async_copy(mask_rows, rows, sems.at[4])
    get_mask.start()
    copies = []
    for i, (src, tile) in enumerate(((state, last), (target, last), (state, 0), (target, 0))):
        copy = pltpu.make_async_copy(src.at[:, tile * 16 : tile * 16 + 16, :], tiles.at[i], sems.at[i])
        copy.start()
        copies.append(copy)
    get_top = pltpu.make_async_copy(target.at[target.shape[0] - 1], top, sems.at[5])
    get_top.start()
    get_mask.wait()
    turned = turn_mask(rows)
    for out, first in ((low, width - 3), (high, 0)):
        m = [jnp.broadcast_to(turned[:, c : c + 1], (64, 128)).astype(BF16) for c in range(first, first + 3)]
        out[256:320, :] = jnp.concatenate([m[0], m[1]], axis=1)
        out[320:384, :] = jnp.concatenate([m[2], m[2]], axis=1)

    def columns(i, half):
        copies[i].wait()

        def step(r, carry):
            v = tiles[i, r].astype(F32)[half * 8 : half * 8 + 8, :]
            at = pl.ds(pl.multiple_of(r * 8, 8), 8)
            part_low[at, :] = v[:, 0:128]
            part_high[at, :] = v[:, 128:256]
            return carry

        lax.fori_loop(0, 64, step, 0, unroll=8)

    for i, (out, half, inner, side) in enumerate(((low, 1, 5, 7), (high, 0, 0, 0))):
        columns(2 * i, half)
        for j in range(3):
            out[j * 64 : j * 64 + 64, :] = strided(part_low, part_high, inner + j, 8).astype(BF16)
        columns(2 * i + 1, half)
        out[192:256, :] = strided(part_low, part_high, side, 8).astype(BF16)
    get_top.wait()


def build_kernel(width, state, mask_rows, in3, mask, low, high):
    turned = turn_mask(mask_rows)
    for c in range(width):
        mask[c * 64 : c * 64 + 64, :] = jnp.broadcast_to(turned[:, c : c + 1], (64, 128))
    widen(state, low, high)

    def own(c, carry):
        put(in3, c + 3, strided(low, high, c, width) * twice(mask[span(c, 1), :]), 0.0)
        return carry

    lax.fori_loop(0, width, own, 0, unroll=4)


def side_mask(side, j):
    lane = (j % 2) * 128
    first = (4 + j // 2) * 64
    return side[first : first + 64, lane : lane + 128].astype(F32)


def side_column(side, j):
    return side[j * 64 : j * 64 + 64, :].astype(F32) * twice(side_mask(side, j))


def flip(rows, used):
    i = lax.broadcasted_iota(jnp.int32, (64, rows.shape[0]), 0)
    k = lax.broadcasted_iota(jnp.int32, (64, rows.shape[0]), 1)
    matrix = jnp.where((i + k == used - 1), 1.0, 0.0).astype(BF16)
    return jnp.dot(matrix, rows, preferred_element_type=F32)


STRIP = 56


def strip_kernel(width, low, high, state, mask, top, out, work):
    work[...] = jnp.zeros_like(work)
    at_mask, at_target = 3 * STRIP, 4 * STRIP
    for side, first in ((low, 0), (high, width + 3)):
        for j in range(3):
            m = side_mask(side, j)
            v = side[j * 64 : j * 64 + 64, :].astype(F32) * twice(m)
            for a in range(3):
                work[a * STRIP + first + j : a * STRIP + first + j + 1, :] = v[61 + a : 62 + a, :]
            work[at_mask + first + j : at_mask + first + j + 1, :] = jnp.concatenate(
                [m[62:63, :], m[63:64, :]], axis=1
            )
    work[at_target + 2 : at_target + 3, :] = low[240:256, :].astype(F32)[15:16, :]
    work[at_target + width + 3 : at_target + width + 4, :] = high[240:256, :].astype(F32)[15:16, :]
    masks = [mask[pl.ds(61 + a, width, stride=64), :] for a in range(3)]
    for a in range(3):
        v = state[(61 + a) * width : (62 + a) * width, :].astype(F32)
        work[a * STRIP + 3 : a * STRIP + 3 + width, :] = v * twice(masks[a])
    work[at_mask + 3 : at_mask + 3 + width, :] = jnp.concatenate([masks[1], masks[2]], axis=1)
    work[at_target + 3 : at_target + 3 + width, :] = top[...].astype(F32)
    out[...] = work[...].astype(BF16)


def conv_kernel(width, in3, w_one, acc):
    n = (width - 2) // 2
    for j in range(2):
        acc[j * n * 64 : (j + 1) * n * 64, :] = jnp.dot(
            tap_rows(in3, 3 + j * n, n), w_one[...], preferred_element_type=F32
        )


def forward_kernel(scale, width, acc, in3_in, target, mask, low, high, strip, strip_own,
                   w_one, w_two, pred, err3, slope, hid3, north, in3, t_low, t_high, p_low, p_high,
                   fix, hid_north, acc_a, acc_b, rows3, north_mask, north_target):
    del in3_in
    widen(target, t_low, t_high)
    top = lax.broadcasted_iota(jnp.int32, (64, 256), 0) == 63
    last = lax.broadcasted_iota(jnp.int32, (16, 256), 0) == 15
    blank = jnp.zeros((8, 256), F32)
    for a in range(4):
        rows3[a, 64:72, :] = blank
    for a in range(3):
        hid_north[a] = jnp.zeros((72, 256), F32)
        rows3[a, 0:64, :] = flip(strip[a * STRIP : (a + 1) * STRIP, :], width + 6)
    rows3[3, 0:64, :] = jnp.zeros((64, 256), F32)
    rows3[3, 0:STRIP, :] = strip_own[2 * STRIP : 3 * STRIP, :].astype(F32)
    for ref, a in ((north_mask, 3), (north_target, 4)):
        ref[64:72, :] = blank
        ref[0:64, :] = flip(strip[a * STRIP : (a + 1) * STRIP, :], width + 6)
    for j in range(3):
        put(in3, j, side_column(low, j), rows3[2, j : j + 1, :])
        k = width + 3 + j
        put(in3, k, side_column(high, j), rows3[2, k : k + 1, :])
    for c in range(width):
        at = pl.ds((c + 3) * 64 + 48, 16)
        rows = in3[2, at, :].astype(F32)
        in3[2, at, :] = jnp.where(last, rows3[2, pl.ds(c + 3, 1), :], rows).astype(BF16)

    def mask_at(col):
        if col < 2:
            return twice(side_mask(low, col + 1))
        if col >= width + 2:
            return twice(side_mask(high, col - width - 2))
        return twice(mask[(col - 2) * 64 : (col - 1) * 64, :])

    def moved(ref, first):
        return jnp.concatenate(
            [ref[first + a, pl.ds(2 - b, 64), :].astype(BF16) for a in range(3) for b in range(3)], axis=1
        )

    lhs = jnp.concatenate([rows3[2, pl.ds(2 + b, 64), :].astype(BF16) for b in range(3)], axis=1)
    fix[...] = jnp.dot(lhs, w_one[6 * 256 : 9 * 256, :], preferred_element_type=F32)
    lhs = jnp.concatenate(
        [tap_rows(in3, 0, 3), tap_rows(in3, width + 1, 3), moved(rows3, 0), moved(rows3, 1)], axis=0
    )
    acc_a[...] = jnp.dot(lhs, w_one[...], preferred_element_type=F32)
    for a in range(2):
        u = acc_a[(6 + a) * 64 : (7 + a) * 64, :].astype(BF16).astype(F32)
        m = twice(north_mask[1:65, a * 128 : a * 128 + 128])
        hid_north[a, 0:64, :] = (gelu_pair(u)[0] * m).astype(BF16).astype(F32)

    def act(col):
        c = col - 2
        if c < 1:
            u = acc_a[col * 64 : col * 64 + 64, :]
        elif c > width - 2:
            k = c - (width - 1) + 3
            u = acc_a[k * 64 : k * 64 + 64, :]
        else:
            u = acc[(c - 1) * 64 : c * 64, :] + jnp.where(top, fix[pl.ds(c, 1), :], 0.0)
        u = u.astype(BF16).astype(F32)
        m = mask_at(col)
        value, grad = gelu_pair(u)
        if 0 <= c < width:
            slope[c * 64 : c * 64 + 64, :] = (grad * m).astype(BF16)
        h = (value * m).astype(BF16).astype(F32)
        hid_north[2, col : col + 1, :] = h[63:64, :]
        put(hid3, col, h, hid_north[1, pl.ds(col, 1), :])

    def loss(e, o):
        c = e - 1
        m = mask_at(e + 1)
        if c < 0:
            t = low[192:256, :].astype(F32)
        elif c >= width:
            t = high[192:256, :].astype(F32)
        else:
            t = strided(t_low, t_high, c, width)
            p = o * m
            at = pl.ds(c, 64, stride=width)
            p_low[at, :] = p[:, 0:128]
            p_high[at, :] = p[:, 128:256]
        v = (m * (o - t) * scale).astype(BF16).astype(F32)
        up, down = shifted(v, 0.0)
        err3[0, span(e, 1), :] = down.astype(BF16)
        err3[1, span(e, 1), :] = v.astype(BF16)
        err3[2, span(e, 1), :] = up.astype(BF16)

    n = 10
    blocks = (width + 2) // n
    done = 0
    for j in range(blocks):
        while done < min(j * n + n + 2, width + 4):
            act(done)
            done += 1
        lhs = tap_rows(hid3, j * n, n)
        rows = n * 64
        if j == blocks - 1:
            lhs = jnp.concatenate([lhs, moved(hid_north, 0)], axis=0)
            rows += 64
        acc_b[j % 2, 0:rows, :] = jnp.dot(lhs, w_two[...], preferred_element_type=F32)
        if j:
            for i in range(n):
                loss((j - 1) * n + i, acc_b[(j - 1) % 2, i * 64 : i * 64 + 64, :])
    for i in range(n):
        loss((blocks - 1) * n + i, acc_b[(blocks - 1) % 2, i * 64 : i * 64 + 64, :])

    o = acc_b[(blocks - 1) % 2, n * 64 : n * 64 + 64, :]
    m = twice(north_mask[2:66, 128:256])
    north[0:64, :] = (m * (o - north_target[2:66, :]) * scale).astype(BF16).astype(F32)
    north[64:72, :] = blank

    def narrow(i, carry):
        at = pl.ds(pl.multiple_of(i * 192, 192), 192)
        pred[at, 0:128] = p_low[at, :].astype(BF16)
        pred[at, 128:256] = p_high[at, :].astype(BF16)
        return carry

    lax.fori_loop(0, pred.shape[0] // 192, narrow, 0)


def tap(field, col, t, rows):
    at = pl.ds(pl.multiple_of((col + t % 3) * 64, 64), rows.shape[0])
    return lax.dot_general(
        field[t // 3, at, :], rows[...], (((0,), (0,)), ((), ())), preferred_element_type=F32
    )


def outer_sent(field, col, rows, send, rest):
    first_core = lax.axis_index("lon") % 2 == 0
    at = jnp.where(first_core, 128, 0)
    for i in range(4):
        r = tap(field, col, i + jnp.where(first_core, 5, 0), rows)
        send[pl.ds(pl.multiple_of(at + i * 256, 128), 256), :] = r.astype(BF16)
    r = tap(field, col, 4, rows)
    end = pl.ds(pl.multiple_of(jnp.where(first_core, 0, 1024), 128), 128)
    send[end, :] = jnp.where(first_core, r[128:256, :], r[0:128, :]).astype(BF16)
    rest[...] = jnp.where(first_core, r[0:128, :], r[128:256, :]).astype(BF16)


def outer_kept(field, col, rows, rest, keep):
    first_core = lax.axis_index("lon") % 2 == 0
    at = jnp.where(first_core, 0, 128)
    for i in range(4):
        r = tap(field, col, i + jnp.where(first_core, 0, 5), rows)
        keep[pl.ds(pl.multiple_of(at + i * 256, 128), 256), :] = r.astype(BF16)
    end = pl.ds(pl.multiple_of(jnp.where(first_core, 1024, 0), 128), 128)
    keep[end, :] = rest[...]


def two_sent_kernel(width, hid3, err3, send, rest):
    outer_sent(hid3, 1, err3.at[1, 64 : 64 + width * 64], send, rest)


def two_kept_kernel(width, hid3, err3, rest, keep):
    outer_kept(hid3, 1, err3.at[1, 64 : 64 + width * 64], rest, keep)


def one_sent_kernel(in3, pre, send, rest):
    outer_sent(in3, 2, pre, send, rest)


def one_kept_kernel(in3, pre, rest, keep):
    outer_kept(in3, 2, pre, rest, keep)


def back_kernel(width, err3, north, slope, w_two, tie, out, w_turned, fold):
    del tie
    for k in range(9):
        w_turned[k * 256 : k * 256 + 256, :] = w_two[k * 256 : k * 256 + 256, :].T
    lhs = jnp.concatenate([north[pl.ds(b, 64), :].astype(BF16) for b in range(3)], axis=1)
    fold[...] = jnp.dot(lhs, w_turned[6 * 256 : 9 * 256, :], preferred_element_type=F32)
    n = 16
    at_top = lax.broadcasted_iota(jnp.int32, (64, 256), 0) == 63
    for j in range(width // n):
        lhs = jnp.concatenate(
            [err3[a, span(j * n + 2 - b, n), :] for a in range(3) for b in range(3)], axis=1
        )
        g = jnp.dot(lhs, w_turned[...], preferred_element_type=F32)
        for i in range(n):
            c = j * n + i
            v = g[i * 64 : i * 64 + 64, :] + jnp.where(at_top, fold[pl.ds(c, 1), :], 0.0)
            out[span(c, 1), :] = (v * slope[span(c, 1), :].astype(F32)).astype(BF16)


def split_kernel(peers, kept, got, *refs):
    *parts, work = refs
    place = (lax.axis_index("lon") // 2) % peers
    rows = parts[0].shape[0]
    work[...] = (kept[...].astype(F32) + got[...].astype(F32)).astype(BF16)
    for k, ref in enumerate(parts):
        ref[...] = work[pl.ds(pl.multiple_of((place ^ k) * rows, rows), rows), :]


def gather_kernel(mine, part_three, part_one, part_two, whole):
    place = (lax.axis_index("lon") // 2) % 4
    rows = mine.shape[0]
    for k, ref in ((0, mine), (3, part_three), (1, part_one), (2, part_two)):
        whole[pl.ds(pl.multiple_of((place ^ k) * rows, rows), rows), :] = ref[...]


def finish_kernel(other_half, half, *refs):
    out, work, sems = refs[-3:]
    core = lax.axis_index("lon") % 2
    core = 1 - core if other_half else core
    rows = half.shape[0]
    chunk = rows // 3
    copies = []
    for i in range(3):
        at = slice(i * chunk, (i + 1) * chunk)
        work[at, :] = half[at, :].astype(F32)
        to = pl.ds(pl.multiple_of(core * rows + i * chunk, chunk), chunk)
        copy = pltpu.make_async_copy(work.at[at, :], out.at[to, :], sems.at[i])
        copy.start()
        copies.append(copy)
    for copy in copies:
        copy.wait()


VMEM = pl.BlockSpec(memory_space=pltpu.VMEM)
ANY = pl.BlockSpec(memory_space=pl.ANY)
HBM = pl.BlockSpec(memory_space=pltpu.HBM)


def call(kernel, args, outs, scratch, flops, grant, alias=None, free=(), free_out=False, away=()):
    outs = [jax.ShapeDtypeStruct(s, d) for s, d in outs]
    size = sum(x.size * x.dtype.itemsize for x in list(args) + outs)
    return pl.pallas_call(
        kernel,
        out_shape=outs,
        in_specs=[ANY if i in free else HBM if i in away else VMEM for i in range(len(args))],
        out_specs=[ANY if free_out else VMEM] * len(outs),
        scratch_shapes=[pltpu.VMEM(*s) if isinstance(s, tuple) else s for s in scratch],
        input_output_aliases=alias or {},
        compiler_params=pltpu.CompilerParams(vmem_limit_bytes=grant << 20),
        cost_estimate=pl.CostEstimate(flops=flops, bytes_accessed=size, transcendentals=0),
    )(*args)


def shift(x, pairs):
    return lax.ppermute(x, "lon", pairs)


def exchange(x, bits, count):
    return shift(x, [(i, i ^ bits) for i in range(count)])


def plus(x, *others):
    total = x.astype(F32)
    for y in others:
        total = total + y.astype(F32)
    return total.astype(BF16)


def split(keep, got, peers):
    half, channels = keep.shape
    return call(
        functools.partial(split_kernel, peers), (keep, got),
        [((half // peers, channels), BF16)] * peers, [((half, channels), BF16)], half * channels, 4,
    )


def along_line(x, count):
    bits = 8
    while bits < count:
        x = plus(x, exchange(x, bits, count))
        bits *= 2
    return x


def finish(mine, other):
    half, channels = mine.shape
    scratch = [((half, channels), F32), pltpu.SemaphoreType.DMA((3,))]
    out = [((2 * half, channels), F32)]
    (total,) = call(
        functools.partial(finish_kernel, False), (mine,), out, scratch,
        half * channels, 4, free_out=True,
    )
    (total,) = call(
        functools.partial(finish_kernel, True), (other, total), out, scratch,
        half * channels, 4, alias={1: 0}, free=(1,), free_out=True,
    )
    return total


def sum_square(keep, got, count):
    own, *parts = split(keep, got, 4)
    got = [exchange(parts[k - 1], 2 * k, count) for k in (3, 1, 2)]
    x = along_line(plus(own, *got), count)
    got = [exchange(x, 2 * k, count) for k in (3, 1, 2)]
    (whole,) = call(gather_kernel, (x, *got), [(keep.shape, BF16)], [], keep.size, 4)
    return finish(whole, exchange(whole, 1, count))


def program(state_in, target, ocean_mask, kernel_one, kernel_two):
    height, width, channels = state_in.shape
    count = lax.axis_size("lon")
    right = [(i, (i + 1) % count) for i in range(count)]
    left = [(i, (i - 1) % count) for i in range(count)]
    mirror = [(i, count - 1 - i) for i in range(count)]
    cells = height * width
    w_one = kernel_one.reshape(9 * channels, channels)
    w_two = kernel_two.reshape(9 * channels, channels)
    unit = 2 * cells * 9 * channels * channels
    scale = 1.0 / math.sqrt(height * width * count)

    state = state_in.reshape(cells, channels)
    target = target.reshape(cells, channels)
    low, high, top = call(
        functools.partial(pack_kernel, width),
        tuple(
            pltpu.with_memory_space_constraint(x, pltpu.HBM)
            for x in (state_in, target.reshape(state_in.shape), ocean_mask.T)
        ),
        [((6 * height, channels), BF16)] * 2 + [((width, channels), BF16)],
        [((4, height, 16, channels), BF16), ((width, height), jnp.int32)]
        + [((8 * height, 128), F32)] * 2 + [pltpu.SemaphoreType.DMA((6,))],
        unit // 16, 8, away=(0, 1, 2),
    )
    low = shift(low, right)
    high = shift(high, left)
    in3, mask = call(
        functools.partial(build_kernel, width), (state, ocean_mask.T),
        [((3, (width + 6) * height, channels), BF16), ((cells, 128), F32)],
        [((cells, 128), F32), ((cells, 128), F32)], unit // 4, 8,
    )
    (strip_own,) = call(
        functools.partial(strip_kernel, width), (low, high, state, mask, top),
        [((5 * STRIP, channels), BF16)], [((5 * STRIP, channels), F32)], unit // 16, 4,
    )
    strip = shift(strip_own, mirror)
    (acc,) = call(
        functools.partial(conv_kernel, width), (in3, w_one),
        [(((width - 2) * height, channels), F32)], [], unit, 6,
    )
    pred, err3, slope, hid3, north, in3 = call(
        functools.partial(forward_kernel, scale, width),
        (acc, in3, target, mask, low, high, strip, strip_own, w_one, w_two),
        [((cells, channels), BF16), ((3, (width + 2) * height, channels), BF16),
         ((cells, channels), BF16), ((3, (width + 4) * height, channels), BF16),
         ((72, channels), F32), (in3.shape, BF16)],
        [((cells, 128), F32)] * 4
        + [((64, channels), F32), ((3, 72, channels), F32), ((512, channels), F32),
           ((2, 704, channels), F32), ((4, 72, channels), F32), ((72, channels), F32),
           ((72, channels), F32)],
        2 * unit, 16, alias={1: 5},
    )
    half = ((9 * channels // 2, channels), BF16)
    rest = ((channels // 2, channels), BF16)
    send, tail = call(
        functools.partial(two_sent_kernel, width), (hid3, err3), [half, rest], [],
        unit // 2, 6,
    )
    got_two = exchange(send, 1, count)
    (keep_two,) = call(
        functools.partial(two_kept_kernel, width), (hid3, err3, tail), [half], [],
        unit // 2, 6,
    )
    (pre,) = call(
        functools.partial(back_kernel, width), (err3, north, slope, w_two, keep_two),
        [((cells, channels), BF16)],
        [((9 * channels, channels), BF16), ((64, channels), F32)],
        unit, 10, free=(4,),
    )
    send, tail = call(one_sent_kernel, (in3, pre), [half, rest], [], unit // 2, 6)
    got_one = exchange(send, 1, count)
    (keep_one,) = call(one_kept_kernel, (in3, pre, tail), [half], [], unit // 2, 6)
    shape = (3, 3, channels, channels)
    grad_two = sum_square(keep_two, got_two, count).reshape(shape)
    grad_one = sum_square(keep_one, got_one, count).reshape(shape)
    return (pred.reshape(height, width, channels), grad_one, grad_two)


def solution(mesh):
    return jax.shard_map(
        program,
        mesh=mesh,
        in_specs=(P("groups", "lon", None), P("groups", "lon", None), P("groups", "lon"), P(), P()),
        out_specs=(
            P("groups", "lon", None),
            P("groups", None, None, None),
            P("groups", None, None, None),
        ),
        check_vma=False,
    )
```

```python
import functools
import math

import jax
import jax.numpy as jnp
from jax import lax
from jax.experimental import pallas as pl
from jax.experimental.pallas import tpu as pltpu
from jax.sharding import PartitionSpec as P


F32 = jnp.float32
BF16 = jnp.bfloat16

ERF_NUM = (
    0.00022905065861350646,
    0.0034082910107109506,
    0.050955695062380861,
    0.18520832239976145,
    1.128379143519084,
)
ERF_DEN = (
    -1.1791602954361697e-7,
    0.000023547966471313185,
    0.0010179625278914885,
    0.014070470171167667,
    0.11098505178285362,
    0.49746925110067538,
    1.0,
)


def erf(x):
    x = jnp.clip(x, -3.832506856900711, 3.832506856900711)
    s = x * x
    num = jnp.full_like(s, ERF_NUM[0])
    for k in ERF_NUM[1:]:
        num = num * s + k
    den = jnp.full_like(s, ERF_DEN[0])
    for k in ERF_DEN[1:]:
        den = den * s + k
    return x * num / den


def gelu_pair(u):
    x = u * math.sqrt(0.5)
    half = 0.5 + 0.5 * erf(x)
    return u * half, half + u * (jnp.exp(-(x * x)) * (1.0 / math.sqrt(2.0 * math.pi)))


def twice(m):
    return jnp.concatenate([m, m], axis=1)


def span(start, size, step=64):
    return pl.ds(pl.multiple_of(start * step, step), size * step)


def tap_rows(ref, col, cols):
    return jnp.concatenate(
        [ref[a, span(col + b, cols), :] for a in range(3) for b in range(3)], axis=1
    )


def shifted(v, north):
    rows = v.shape[0]
    at = lax.broadcasted_iota(jnp.int32, (8, v.shape[1]), 0)
    up = pltpu.roll(v, 1, 0)
    down = pltpu.roll(v, rows - 1, 0)
    up = jnp.concatenate([jnp.where(at == 0, 0.0, up[0:8, :]), up[8:rows, :]], axis=0)
    down = jnp.concatenate(
        [down[0 : rows - 8, :], jnp.where(at == 7, north, down[rows - 8 : rows, :])], axis=0
    )
    return up, down


def strided(low, high, col, width):
    at = pl.ds(col, 64, stride=width)
    return jnp.concatenate([low[at, :], high[at, :]], axis=1)


def widen(src, low, high):
    rows = 192

    def step(i, carry):
        at = pl.ds(pl.multiple_of(i * rows, rows), rows)
        low[at, :] = src[at, 0:128].astype(F32)
        high[at, :] = src[at, 128:256].astype(F32)
        return carry

    lax.fori_loop(0, src.shape[0] // rows, step, 0)


def put(ref, col, v, north):
    up, down = shifted(v, north)
    ref[0, span(col, 1), :] = up.astype(BF16)
    ref[1, span(col, 1), :] = v.astype(BF16)
    ref[2, span(col, 1), :] = down.astype(BF16)


def turn_mask(mask_rows):
    blank = jnp.zeros((128 - mask_rows.shape[0], 64), jnp.int32)
    return jnp.concatenate([mask_rows[...], blank], axis=0).astype(F32).T


def pack_kernel(width, state, target, mask_rows, low, high, top, tiles, rows, part_low, part_high, sems):
    last = width // 16 - 1
    get_mask = pltpu.make_async_copy(mask_rows, rows, sems.at[4])
    get_mask.start()
    copies = []
    for i, (src, tile) in enumerate(((state, last), (target, last), (state, 0), (target, 0))):
        copy = pltpu.make_async_copy(src.at[:, tile * 16 : tile * 16 + 16, :], tiles.at[i], sems.at[i])
        copy.start()
        copies.append(copy)
    get_top = pltpu.make_async_copy(target.at[target.shape[0] - 1], top, sems.at[5])
    get_top.start()
    get_mask.wait()
    turned = turn_mask(rows)
    for out, first in ((low, width - 3), (high, 0)):
        m = [jnp.broadcast_to(turned[:, c : c + 1], (64, 128)).astype(BF16) for c in range(first, first + 3)]
        out[256:320, :] = jnp.concatenate([m[0], m[1]], axis=1)
        out[320:384, :] = jnp.concatenate([m[2], m[2]], axis=1)

    def columns(i, half):
        copies[i].wait()

        def step(r, carry):
            v = tiles[i, r].astype(F32)[half * 8 : half * 8 + 8, :]
            at = pl.ds(pl.multiple_of(r * 8, 8), 8)
            part_low[at, :] = v[:, 0:128]
            part_high[at, :] = v[:, 128:256]
            return carry

        lax.fori_loop(0, 64, step, 0, unroll=8)

    for i, (out, half, inner, side) in enumerate(((low, 1, 5, 7), (high, 0, 0, 0))):
        columns(2 * i, half)
        for j in range(3):
            out[j * 64 : j * 64 + 64, :] = strided(part_low, part_high, inner + j, 8).astype(BF16)
        columns(2 * i + 1, half)
        out[192:256, :] = strided(part_low, part_high, side, 8).astype(BF16)
    get_top.wait()


def build_kernel(width, state, mask_rows, in3, mask, low, high):
    turned = turn_mask(mask_rows)
    for c in range(width):
        mask[c * 64 : c * 64 + 64, :] = jnp.broadcast_to(turned[:, c : c + 1], (64, 128))
    widen(state, low, high)

    def own(c, carry):
        put(in3, c + 3, strided(low, high, c, width) * twice(mask[span(c, 1), :]), 0.0)
        return carry

    lax.fori_loop(0, width, own, 0, unroll=4)


def side_mask(side, j):
    lane = (j % 2) * 128
    first = (4 + j // 2) * 64
    return side[first : first + 64, lane : lane + 128].astype(F32)


def side_column(side, j):
    return side[j * 64 : j * 64 + 64, :].astype(F32) * twice(side_mask(side, j))


def flip(rows, used):
    i = lax.broadcasted_iota(jnp.int32, (64, rows.shape[0]), 0)
    k = lax.broadcasted_iota(jnp.int32, (64, rows.shape[0]), 1)
    matrix = jnp.where((i + k == used - 1), 1.0, 0.0).astype(BF16)
    return jnp.dot(matrix, rows, preferred_element_type=F32)


STRIP = 56


def strip_kernel(width, low, high, state, mask, top, out, work):
    work[...] = jnp.zeros_like(work)
    at_mask, at_target = 3 * STRIP, 4 * STRIP
    for side, first in ((low, 0), (high, width + 3)):
        for j in range(3):
            m = side_mask(side, j)
            v = side[j * 64 : j * 64 + 64, :].astype(F32) * twice(m)
            for a in range(3):
                work[a * STRIP + first + j : a * STRIP + first + j + 1, :] = v[61 + a : 62 + a, :]
            work[at_mask + first + j : at_mask + first + j + 1, :] = jnp.concatenate(
                [m[62:63, :], m[63:64, :]], axis=1
            )
    work[at_target + 2 : at_target + 3, :] = low[240:256, :].astype(F32)[15:16, :]
    work[at_target + width + 3 : at_target + width + 4, :] = high[240:256, :].astype(F32)[15:16, :]
    masks = [mask[pl.ds(61 + a, width, stride=64), :] for a in range(3)]
    for a in range(3):
        v = state[(61 + a) * width : (62 + a) * width, :].astype(F32)
        work[a * STRIP + 3 : a * STRIP + 3 + width, :] = v * twice(masks[a])
    work[at_mask + 3 : at_mask + 3 + width, :] = jnp.concatenate([masks[1], masks[2]], axis=1)
    work[at_target + 3 : at_target + 3 + width, :] = top[...].astype(F32)
    out[...] = work[...].astype(BF16)


def conv_kernel(width, in3, w_one, acc):
    n = (width - 2) // 2
    for j in range(2):
        acc[j * n * 64 : (j + 1) * n * 64, :] = jnp.dot(
            tap_rows(in3, 3 + j * n, n), w_one[...], preferred_element_type=F32
        )


def forward_kernel(scale, width, acc, in3_in, target, mask, low, high, strip, strip_own,
                   w_one, w_two, pred, err3, slope, hid3, north, in3, t_low, t_high, p_low, p_high,
                   fix, hid_north, acc_a, acc_b, rows3, north_mask, north_target):
    del in3_in
    widen(target, t_low, t_high)
    top = lax.broadcasted_iota(jnp.int32, (8, 256), 0) == 7
    last = lax.broadcasted_iota(jnp.int32, (16, 256), 0) == 15
    blank = jnp.zeros((8, 256), F32)
    for a in range(4):
        rows3[a, 64:72, :] = blank
    for a in range(3):
        hid_north[a] = jnp.zeros((72, 256), F32)
        rows3[a, 0:64, :] = flip(strip[a * STRIP : (a + 1) * STRIP, :], width + 6)
    rows3[3, 0:64, :] = jnp.zeros((64, 256), F32)
    rows3[3, 0:STRIP, :] = strip_own[2 * STRIP : 3 * STRIP, :].astype(F32)
    for ref, a in ((north_mask, 3), (north_target, 4)):
        ref[64:72, :] = blank
        ref[0:64, :] = flip(strip[a * STRIP : (a + 1) * STRIP, :], width + 6)
    for j in range(3):
        put(in3, j, side_column(low, j), rows3[2, j : j + 1, :])
        k = width + 3 + j
        put(in3, k, side_column(high, j), rows3[2, k : k + 1, :])
    for c in range(width):
        at = pl.ds((c + 3) * 64 + 48, 16)
        rows = in3[2, at, :].astype(F32)
        in3[2, at, :] = jnp.where(last, rows3[2, pl.ds(c + 3, 1), :], rows).astype(BF16)

    def mask_at(col):
        if col < 2:
            return twice(side_mask(low, col + 1))
        if col >= width + 2:
            return twice(side_mask(high, col - width - 2))
        return twice(mask[(col - 2) * 64 : (col - 1) * 64, :])

    def moved(ref, first):
        return jnp.concatenate(
            [ref[first + a, pl.ds(2 - b, 64), :].astype(BF16) for a in range(3) for b in range(3)], axis=1
        )

    lhs = jnp.concatenate([rows3[2, pl.ds(2 + b, 64), :].astype(BF16) for b in range(3)], axis=1)
    fix[...] = jnp.dot(lhs, w_one[6 * 256 : 9 * 256, :], preferred_element_type=F32)
    lhs = jnp.concatenate(
        [tap_rows(in3, 0, 3), tap_rows(in3, width + 1, 3), moved(rows3, 0), moved(rows3, 1)], axis=0
    )
    acc_a[...] = jnp.dot(lhs, w_one[...], preferred_element_type=F32)
    for a in range(2):
        u = acc_a[(6 + a) * 64 : (7 + a) * 64, :].astype(BF16).astype(F32)
        m = twice(north_mask[1:65, a * 128 : a * 128 + 128])
        hid_north[a, 0:64, :] = (gelu_pair(u)[0] * m).astype(BF16).astype(F32)

    def act(col):
        c = col - 2
        if c < 1:
            u = acc_a[col * 64 : col * 64 + 64, :]
        elif c > width - 2:
            k = c - (width - 1) + 3
            u = acc_a[k * 64 : k * 64 + 64, :]
        else:
            u = acc[(c - 1) * 64 : c * 64, :]
            u = jnp.concatenate(
                [u[0:56, :], u[56:64, :] + jnp.where(top, fix[pl.ds(c, 1), :], 0.0)], axis=0
            )
        u = u.astype(BF16).astype(F32)
        m = mask_at(col)
        value, grad = gelu_pair(u)
        if 0 <= c < width:
            slope[c * 64 : c * 64 + 64, :] = (grad * m).astype(BF16)
        h = (value * m).astype(BF16).astype(F32)
        hid_north[2, col : col + 1, :] = h[63:64, :]
        put(hid3, col, h, hid_north[1, pl.ds(col, 1), :])

    def loss(e, o):
        c = e - 1
        m = mask_at(e + 1)
        if c < 0:
            t = low[192:256, :].astype(F32)
        elif c >= width:
            t = high[192:256, :].astype(F32)
        else:
            t = strided(t_low, t_high, c, width)
            p = o * m
            at = pl.ds(c, 64, stride=width)
            p_low[at, :] = p[:, 0:128]
            p_high[at, :] = p[:, 128:256]
        v = (m * (o - t) * scale).astype(BF16).astype(F32)
        up, down = shifted(v, 0.0)
        err3[0, span(e, 1), :] = down.astype(BF16)
        err3[1, span(e, 1), :] = v.astype(BF16)
        err3[2, span(e, 1), :] = up.astype(BF16)

    n = 5
    blocks = (width + 2) // n
    done = 0
    for j in range(blocks):
        while done < min(j * n + n + 2, width + 4):
            act(done)
            done += 1
        lhs = tap_rows(hid3, j * n, n)
        rows = n * 64
        if j == blocks - 1:
            lhs = jnp.concatenate([lhs, moved(hid_north, 0)], axis=0)
            rows += 64
        acc_b[j % 2, 0:rows, :] = jnp.dot(lhs, w_two[...], preferred_element_type=F32)
        if j:
            for i in range(n):
                loss((j - 1) * n + i, acc_b[(j - 1) % 2, i * 64 : i * 64 + 64, :])
    for i in range(n):
        loss((blocks - 1) * n + i, acc_b[(blocks - 1) % 2, i * 64 : i * 64 + 64, :])

    o = acc_b[(blocks - 1) % 2, n * 64 : n * 64 + 64, :]
    m = twice(north_mask[2:66, 128:256])
    north[0:64, :] = (m * (o - north_target[2:66, :]) * scale).astype(BF16).astype(F32)
    north[64:72, :] = blank

    def narrow(i, carry):
        at = pl.ds(pl.multiple_of(i * 192, 192), 192)
        pred[at, 0:128] = p_low[at, :].astype(BF16)
        pred[at, 128:256] = p_high[at, :].astype(BF16)
        return carry

    lax.fori_loop(0, pred.shape[0] // 192, narrow, 0)


def tap(field, col, t, rows):
    at = pl.ds(pl.multiple_of((col + t % 3) * 64, 64), rows.shape[0])
    return lax.dot_general(
        field[t // 3, at, :], rows[...], (((0,), (0,)), ((), ())), preferred_element_type=F32
    )


def outer_sent(field, col, rows, send, rest):
    first_core = lax.axis_index("lon") % 2 == 0
    at = jnp.where(first_core, 128, 0)
    for i in range(4):
        r = tap(field, col, i + jnp.where(first_core, 5, 0), rows)
        send[pl.ds(pl.multiple_of(at + i * 256, 128), 256), :] = r.astype(BF16)
    r = tap(field, col, 4, rows)
    end = pl.ds(pl.multiple_of(jnp.where(first_core, 0, 1024), 128), 128)
    send[end, :] = jnp.where(first_core, r[128:256, :], r[0:128, :]).astype(BF16)
    rest[...] = jnp.where(first_core, r[0:128, :], r[128:256, :]).astype(BF16)


def outer_kept(field, col, rows, rest, keep):
    first_core = lax.axis_index("lon") % 2 == 0
    at = jnp.where(first_core, 0, 128)
    for i in range(4):
        r = tap(field, col, i + jnp.where(first_core, 0, 5), rows)
        keep[pl.ds(pl.multiple_of(at + i * 256, 128), 256), :] = r.astype(BF16)
    end = pl.ds(pl.multiple_of(jnp.where(first_core, 1024, 0), 128), 128)
    keep[end, :] = rest[...]


def two_sent_kernel(width, hid3, err3, send, rest):
    outer_sent(hid3, 1, err3.at[1, 64 : 64 + width * 64], send, rest)


def two_kept_kernel(width, hid3, err3, rest, keep):
    outer_kept(hid3, 1, err3.at[1, 64 : 64 + width * 64], rest, keep)


def one_sent_kernel(in3, pre, send, rest):
    outer_sent(in3, 2, pre, send, rest)


def one_kept_kernel(in3, pre, rest, keep):
    outer_kept(in3, 2, pre, rest, keep)


def back_kernel(width, err3, north, slope, w_two, tie, out, w_turned, fold):
    del tie
    for k in range(9):
        w_turned[k * 256 : k * 256 + 256, :] = w_two[k * 256 : k * 256 + 256, :].T
    lhs = jnp.concatenate([north[pl.ds(b, 64), :].astype(BF16) for b in range(3)], axis=1)
    fold[...] = jnp.dot(lhs, w_turned[6 * 256 : 9 * 256, :], preferred_element_type=F32)
    n = 16
    at_top = lax.broadcasted_iota(jnp.int32, (64, 256), 0) == 63
    for j in range(width // n):
        lhs = jnp.concatenate(
            [err3[a, span(j * n + 2 - b, n), :] for a in range(3) for b in range(3)], axis=1
        )
        g = jnp.dot(lhs, w_turned[...], preferred_element_type=F32)
        for i in range(n):
            c = j * n + i
            v = g[i * 64 : i * 64 + 64, :] + jnp.where(at_top, fold[pl.ds(c, 1), :], 0.0)
            out[span(c, 1), :] = (v * slope[span(c, 1), :].astype(F32)).astype(BF16)


def split_kernel(peers, kept, got, *refs):
    *parts, work = refs
    place = (lax.axis_index("lon") // 2) % peers
    rows = parts[0].shape[0]
    work[...] = (kept[...].astype(F32) + got[...].astype(F32)).astype(BF16)
    for k, ref in enumerate(parts):
        ref[...] = work[pl.ds(pl.multiple_of((place ^ k) * rows, rows), rows), :]


def gather_kernel(mine, part_three, part_one, part_two, whole):
    place = (lax.axis_index("lon") // 2) % 4
    rows = mine.shape[0]
    for k, ref in ((0, mine), (3, part_three), (1, part_one), (2, part_two)):
        whole[pl.ds(pl.multiple_of((place ^ k) * rows, rows), rows), :] = ref[...]


def finish_kernel(other_half, half, *refs):
    out, work, sems = refs[-3:]
    core = lax.axis_index("lon") % 2
    core = 1 - core if other_half else core
    rows = half.shape[0]
    chunk = rows // 3
    copies = []
    for i in range(3):
        at = slice(i * chunk, (i + 1) * chunk)
        work[at, :] = half[at, :].astype(F32)
        to = pl.ds(pl.multiple_of(core * rows + i * chunk, chunk), chunk)
        copy = pltpu.make_async_copy(work.at[at, :], out.at[to, :], sems.at[i])
        copy.start()
        copies.append(copy)
    for copy in copies:
        copy.wait()


VMEM = pl.BlockSpec(memory_space=pltpu.VMEM)
ANY = pl.BlockSpec(memory_space=pl.ANY)
HBM = pl.BlockSpec(memory_space=pltpu.HBM)


def call(kernel, args, outs, scratch, flops, grant, alias=None, free=(), free_out=False, away=()):
    outs = [jax.ShapeDtypeStruct(s, d) for s, d in outs]
    size = sum(x.size * x.dtype.itemsize for x in list(args) + outs)
    return pl.pallas_call(
        kernel,
        out_shape=outs,
        in_specs=[ANY if i in free else HBM if i in away else VMEM for i in range(len(args))],
        out_specs=[ANY if free_out else VMEM] * len(outs),
        scratch_shapes=[pltpu.VMEM(*s) if isinstance(s, tuple) else s for s in scratch],
        input_output_aliases=alias or {},
        compiler_params=pltpu.CompilerParams(vmem_limit_bytes=grant << 20),
        cost_estimate=pl.CostEstimate(flops=flops, bytes_accessed=size, transcendentals=0),
    )(*args)


def shift(x, pairs):
    return lax.ppermute(x, "lon", pairs)


def exchange(x, bits, count):
    return shift(x, [(i, i ^ bits) for i in range(count)])


def plus(x, *others):
    total = x.astype(F32)
    for y in others:
        total = total + y.astype(F32)
    return total.astype(BF16)


def split(keep, got, peers):
    half, channels = keep.shape
    return call(
        functools.partial(split_kernel, peers), (keep, got),
        [((half // peers, channels), BF16)] * peers, [((half, channels), BF16)], half * channels, 4,
    )


def along_line(x, count):
    bits = 8
    while bits < count:
        x = plus(x, exchange(x, bits, count))
        bits *= 2
    return x


def finish(mine, other):
    half, channels = mine.shape
    scratch = [((half, channels), F32), pltpu.SemaphoreType.DMA((3,))]
    out = [((2 * half, channels), F32)]
    (total,) = call(
        functools.partial(finish_kernel, False), (mine,), out, scratch,
        half * channels, 4, free_out=True,
    )
    (total,) = call(
        functools.partial(finish_kernel, True), (other, total), out, scratch,
        half * channels, 4, alias={1: 0}, free=(1,), free_out=True,
    )
    return total


def sum_square(keep, got, count):
    own, *parts = split(keep, got, 4)
    got = [exchange(parts[k - 1], 2 * k, count) for k in (3, 1, 2)]
    x = along_line(plus(own, *got), count)
    got = [exchange(x, 2 * k, count) for k in (3, 1, 2)]
    (whole,) = call(gather_kernel, (x, *got), [(keep.shape, BF16)], [], keep.size, 4)
    return finish(whole, exchange(whole, 1, count))


def program(state_in, target, ocean_mask, kernel_one, kernel_two):
    height, width, channels = state_in.shape
    count = lax.axis_size("lon")
    right = [(i, (i + 1) % count) for i in range(count)]
    left = [(i, (i - 1) % count) for i in range(count)]
    mirror = [(i, count - 1 - i) for i in range(count)]
    cells = height * width
    w_one = kernel_one.reshape(9 * channels, channels)
    w_two = kernel_two.reshape(9 * channels, channels)
    unit = 2 * cells * 9 * channels * channels
    scale = 1.0 / math.sqrt(height * width * count)

    state = state_in.reshape(cells, channels)
    target = target.reshape(cells, channels)
    low, high, top = call(
        functools.partial(pack_kernel, width),
        tuple(
            pltpu.with_memory_space_constraint(x, pltpu.HBM)
            for x in (state_in, target.reshape(state_in.shape), ocean_mask.T)
        ),
        [((6 * height, channels), BF16)] * 2 + [((width, channels), BF16)],
        [((4, height, 16, channels), BF16), ((width, height), jnp.int32)]
        + [((8 * height, 128), F32)] * 2 + [pltpu.SemaphoreType.DMA((6,))],
        unit // 16, 8, away=(0, 1, 2),
    )
    low = shift(low, right)
    high = shift(high, left)
    in3, mask = call(
        functools.partial(build_kernel, width), (state, ocean_mask.T),
        [((3, (width + 6) * height, channels), BF16), ((cells, 128), F32)],
        [((cells, 128), F32), ((cells, 128), F32)], unit // 4, 8,
    )
    (strip_own,) = call(
        functools.partial(strip_kernel, width), (low, high, state, mask, top),
        [((5 * STRIP, channels), BF16)], [((5 * STRIP, channels), F32)], unit // 16, 4,
    )
    strip = shift(strip_own, mirror)
    (acc,) = call(
        functools.partial(conv_kernel, width), (in3, w_one),
        [(((width - 2) * height, channels), F32)], [], unit, 6,
    )
    pred, err3, slope, hid3, north, in3 = call(
        functools.partial(forward_kernel, scale, width),
        (acc, in3, target, mask, low, high, strip, strip_own, w_one, w_two),
        [((cells, channels), BF16), ((3, (width + 2) * height, channels), BF16),
         ((cells, channels), BF16), ((3, (width + 4) * height, channels), BF16),
         ((72, channels), F32), (in3.shape, BF16)],
        [((cells, 128), F32)] * 4
        + [((64, channels), F32), ((3, 72, channels), F32), ((512, channels), F32),
           ((2, 384, channels), F32), ((4, 72, channels), F32), ((72, channels), F32),
           ((72, channels), F32)],
        2 * unit, 16, alias={1: 5},
    )
    half = ((9 * channels // 2, channels), BF16)
    rest = ((channels // 2, channels), BF16)
    send, tail = call(
        functools.partial(two_sent_kernel, width), (hid3, err3), [half, rest], [],
        unit // 2, 6,
    )
    got_two = exchange(send, 1, count)
    (keep_two,) = call(
        functools.partial(two_kept_kernel, width), (hid3, err3, tail), [half], [],
        unit // 2, 6,
    )
    (pre,) = call(
        functools.partial(back_kernel, width), (err3, north, slope, w_two, keep_two),
        [((cells, channels), BF16)],
        [((9 * channels, channels), BF16), ((64, channels), F32)],
        unit, 10, free=(4,),
    )
    send, tail = call(one_sent_kernel, (in3, pre), [half, rest], [], unit // 2, 6)
    got_one = exchange(send, 1, count)
    (keep_one,) = call(one_kept_kernel, (in3, pre, tail), [half], [], unit // 2, 6)
    shape = (3, 3, channels, channels)
    grad_two = sum_square(keep_two, got_two, count).reshape(shape)
    grad_one = sum_square(keep_one, got_one, count).reshape(shape)
    return (pred.reshape(height, width, channels), grad_one, grad_two)


def solution(mesh):
    return jax.shard_map(
        program,
        mesh=mesh,
        in_specs=(P("groups", "lon", None), P("groups", "lon", None), P("groups", "lon"), P(), P()),
        out_specs=(
            P("groups", "lon", None),
            P("groups", None, None, None),
            P("groups", None, None, None),
        ),
        check_vma=False,
    )
```
